32 devices in a mesh: wide: 16 (over z, x, core), narrow: 2 (over y).
Axes of the slice: x: 2, y: 2, z: 4, core: 2. Of those that a mesh axis runs over, the one named last changes fastest.
Arguments:
- activations: bfloat16 [4096, 8192], P('narrow', 'wide'), may hold values from -6 to 6
- cotangent: bfloat16 [4096, 4096], P('wide', 'narrow'), may hold values from -6 to 6
- sign_bits: int32 [8192, 4096], P('wide', 'narrow'), may hold values from 0 to 1
- seg_lengths: int32 [4], replicated, may hold values from 1 to 1536, 4096 in all
- kept_index: int32 [16384], replicated, may hold values from 0 to 33554431
Outputs:
- sketch: float32 [4, 16384], P(None, ('wide', 'narrow'))
The draws below stay inside these ranges and needn't reach their ends.
Inputs may be any that keep to these rules, and one draw needn't show every extreme that they name: `seg_lengths`: the lengths sum to 4096; the longest is exactly 1536.
All inputs are finite; a program needn't handle non-finite values.
Results may differ from the reference program's by a relative error of at most 0.0003.
Values may be sent and summed in bfloat16 or wider, within the bound.
A program may use at most 192 MiB of HBM per device.

```python
import math
import jax
import jax.numpy as jnp
import numpy as np
from jax import lax

D = 8192
H = 4096
KEEP = 16384
SEG = 4
MOST = 1536
TOKENS = 4096
N_WIDE = 16
N_NARROW = 2


def with_ends(entries, stream_key, smallest, top_value):
    longest = entries.shape.index(max(entries.shape))
    spots = []
    for shift in (0, 1):
        where = [jax.random.randint(jax.random.fold_in(stream_key, axis), (), 0, length) for axis, length in enumerate(entries.shape)]
        where[longest] = (where[longest] + shift) % entries.shape[longest]
        spots.append(tuple(where))
    return entries.at[spots[0]].set(smallest).at[spots[1]].set(top_value)


def shard_levels(rng, shape, split, smallest, high):
    gain = 1.0
    for axis_at, blocks in split:
        steps = jax.random.uniform(jax.random.fold_in(jax.random.fold_in(rng, 6), axis_at), (blocks,), jnp.float32, smallest / len(split), high / len(split))
        gain = gain * jnp.repeat(jnp.exp(steps), shape[axis_at] // blocks).reshape((-1,) + (1,) * (len(shape) - 1 - axis_at))
    return gain


def length_profile(number_of, total, reach, slope):
    weights = [(1 << 20) // math.isqrt(grade ** slope) + 1 for grade in range(2, number_of + 1)]
    rest, counts = total - reach - (number_of - 1), [1] * (number_of - 1)
    while rest > 0:
        movable = [i for i in range(number_of - 1) if counts[i] < reach]
        whole, remaining = sum([weights[i] for i in movable]), rest
        for i in movable:
            extra = min(reach - counts[i], max(1, remaining * weights[i] // whole), rest)
            counts[i] = counts[i] + extra
            rest = rest - extra
    return np.array([reach] + counts)


def ragged_sizes(stream_key, amount, total, most, skew):
    if amount == 2:
        one = jax.random.randint(stream_key, (), max(1, total - most), min(most, total - 1) + 1)
        return jnp.stack([one, total - one])
    lengths = jnp.asarray(length_profile(amount, total, most, skew), jnp.int32)
    couples = (amount - 1) // 2
    donor, sink = lengths[1:1 + 2 * couples:2], lengths[2:2 + 2 * couples:2]
    room = jnp.minimum(donor - 1, most - sink)
    passed = jax.random.randint(jax.random.fold_in(stream_key, 1), (couples,), 0, 1 << 20) % (room + 1)
    lengths = lengths.at[1:1 + 2 * couples:2].set(donor - passed).at[2:2 + 2 * couples:2].set(sink + passed)
    return lengths[jax.random.permutation(jax.random.fold_in(stream_key, 2), amount)]


def scatter_about(key, shape, width, bound, split=(), kind=jnp.bfloat16):
    gain = shard_levels(key, shape, split, -0.22, 0.18) if split else 1.0
    values = jax.random.normal(key, shape, jnp.float32) * width * gain
    return jnp.minimum(jnp.maximum(values, -bound), bound).astype(kind)


def setup_inputs(seed: int = 0) -> dict:
    streams_of = jax.random.split(jax.random.key(seed), 6)
    return {
        "activations": scatter_about(streams_of[0], (TOKENS, D), 1.0, 6.0, ((0, 2), (1, 16))),
        "cotangent": scatter_about(streams_of[1], (TOKENS, H), 1.0, 6.0, ((0, 16), (1, 2))),
        "sign_bits": with_ends(jax.random.randint(streams_of[2], (D, H), 0, 2), jax.random.fold_in(streams_of[2], 1), 0, 1).astype(jnp.int32),
        "seg_lengths": ragged_sizes(streams_of[3], SEG, TOKENS, MOST, 1).astype(jnp.int32),
        "kept_index": with_ends(jax.random.randint(streams_of[4], (KEEP,), 0, D * H), jax.random.fold_in(streams_of[4], 1), 0, (D * H) - 1).astype(jnp.int32),
    }


def sylvester(extent):
    indices = jnp.arange(extent, dtype=jnp.int32)
    common = indices[:, None] & indices[None, :]
    parity = jnp.zeros((extent, extent), jnp.int32)
    for bit_pos in range(extent.bit_length() - 1):
        parity = parity + (common >> bit_pos & 1)
    return (1 - 2 * (parity % 2)).astype(jnp.float32)

def reference(activations, cotangent, sign_bits, seg_lengths, kept_index):
    highest = lax.Precision.HIGHEST
    total_tok = activations.shape[0]
    starts = (jnp.cumsum(seg_lengths) - seg_lengths).astype(jnp.int32)
    signs = (1 - 2 * sign_bits).astype(jnp.float32)
    rows_local = D // N_WIDE
    cols_local = H // N_NARROW
    left_local = sylvester(rows_local)
    left_outer = sylvester(N_WIDE)
    right_local = sylvester(cols_local)
    right_outer = sylvester(N_NARROW)
    scale = 1.0 / math.sqrt(D * H)

    def one_segment(packed):
        begin_at, count = packed
        clamped = jnp.minimum(begin_at, total_tok - MOST).astype(jnp.int32)
        rows_x = lax.dynamic_slice_in_dim(activations, clamped, MOST, 0).astype(jnp.float32)
        rows_c = lax.dynamic_slice_in_dim(cotangent, clamped, MOST, 0).astype(jnp.float32)
        where_at = clamped + jnp.arange(MOST, dtype=jnp.int32)
        inside = (where_at >= begin_at) & (where_at < begin_at + count)
        rows_c = jnp.where(inside[:, None], rows_c, jnp.zeros((), jnp.float32))
        grad = jnp.dot(rows_x.T, rows_c, precision=highest)
        signed = grad * lax.rsqrt(count.astype(jnp.float32)) * signs
        blocks = signed.reshape(N_WIDE, rows_local, H)
        blocks = jnp.einsum('ab,wbh->wah', left_local, blocks, precision=highest)
        blocks = jnp.einsum('vw,wah->vah', left_outer, blocks, precision=highest)
        blocks = blocks.reshape(D, N_NARROW, cols_local)
        blocks = jnp.einsum('dnc,ce->dne', blocks, right_local, precision=highest)
        blocks = jnp.einsum('dne,nm->dme', blocks, right_outer, precision=highest)
        return jnp.take(blocks.reshape(-1), kept_index) * scale
    return lax.map(one_segment, (starts, seg_lengths))
```

```python
import functools
import math

import jax
import jax.numpy as jnp
import numpy as np
from jax import lax
from jax.experimental import pallas as pl
from jax.experimental.pallas import tpu as pltpu
from jax.sharding import PartitionSpec as P

LANES = 128
MOST = 1536
MESH = pl.DeviceIdType.MESH


def sylvester(extent):
    indices = np.arange(extent)
    common = indices[:, None] & indices[None, :]
    parity = np.zeros((extent, extent), np.int64)
    for bit_pos in range(extent.bit_length() - 1):
        parity += common >> bit_pos & 1
    return jnp.asarray(1 - 2 * (parity % 2), jnp.bfloat16)


def butterflies(parts):
    parts = list(parts)
    gap = 1
    while gap < len(parts):
        for low in range(len(parts)):
            if not low & gap:
                one, two = parts[low], parts[low | gap]
                parts[low], parts[low | gap] = one + two, one - two
        gap *= 2
    return parts


def halves(values):
    high = values.astype(jnp.bfloat16)
    low = (values - high.astype(jnp.float32)).astype(jnp.bfloat16)
    return high, low


def sketch_kernel(
    n_wide, n_narrow, cross, windows, n_chunks,
    bounds, gains, acts, cots, bits_in, left_ref, right_ref,
    out_ref, acts_all, bits_ref, flipped, table, bufs, grads,
    local_sem, acts_send, acts_recv, cots_send, cots_recv,
):
    wide = lax.axis_index("wide")
    narrow = lax.axis_index("narrow")
    lines = n_wide // (2 * cross)
    core = lax.rem(wide, 2)
    side = lax.rem(wide // 2, cross)
    place = wide // (2 * cross)
    tok_acts = acts.shape[0]
    tok_cots = cots.shape[0]
    rows, cols = bits_in.shape
    row_block = left_ref.shape[0]
    col_block = right_ref.shape[0]
    row_groups = rows // row_block
    per_group = col_block // LANES
    seg_count = len(windows)
    stretch = per_group * rows * seg_count

    def index_of(at, across, on_core):
        return (at * cross + across) * 2 + on_core

    partner = index_of(place, side, 1 - core)
    up = index_of(lax.rem(place + 1, lines), side, core)
    down = index_of(lax.rem(place + lines - 1, lines), side, core)
    across = [lax.rem(side + off, cross) for off in range(1, cross)]
    has_up = place < lines - 1
    has_down = place > 0

    my_acts = pl.ds(narrow * tok_acts, tok_acts)
    my_cots = pl.ds(wide * tok_cots, tok_cots)

    def columns_of(chunk):
        return pl.ds(pl.multiple_of(chunk * col_block, col_block), col_block)

    def own_cots(chunk):
        return pltpu.make_async_copy(
            cots.at[:, columns_of(chunk)], bufs.at[chunk, my_cots, :], local_sem.at[2 + chunk]
        )

    def put_out(chunk):
        span = pl.ds(pl.multiple_of(chunk * stretch, 8), stretch)
        return pltpu.make_async_copy(
            table.at[span, :], out_ref.at[span, :], local_sem.at[2 + n_chunks + chunk]
        )

    own_acts = pltpu.make_async_copy(acts, acts_all.at[my_acts, :], local_sem.at[0])
    own_bits = pltpu.make_async_copy(bits_in, bits_ref, local_sem.at[1])
    for chunk in range(n_chunks):
        own_cots(chunk).start()
    own_acts.start()
    own_bits.start()

    barrier = pltpu.get_barrier_semaphore()

    def greet(**where):
        pl.semaphore_signal(barrier, inc=1, device_id=where, device_id_type=MESH)

    greet(wide=partner)
    for other in across:
        greet(wide=index_of(place, other, core))
    for off in range(1, n_narrow):
        greet(narrow=lax.rem(narrow + off, n_narrow))

    @pl.when(has_up)
    def _():
        greet(wide=up)

    @pl.when(has_down)
    def _():
        greet(wide=down)

    ends = jnp.where(has_up, 1, 0) + jnp.where(has_down, 1, 0)
    pl.semaphore_wait(barrier, 1 + (cross - 1) + (n_narrow - 1) + ends)

    def acts_copy(off):
        return pltpu.make_async_remote_copy(
            src_ref=acts,
            dst_ref=acts_all.at[my_acts, :],
            send_sem=acts_send.at[off],
            recv_sem=acts_recv.at[off],
            device_id={"narrow": lax.rem(narrow + off, n_narrow)},
            device_id_type=MESH,
        )

    def cots_copy(chunk, way, shard, to):
        place_of = bufs.at[chunk, pl.ds(shard * tok_cots, tok_cots), :]
        return pltpu.make_async_remote_copy(
            src_ref=place_of,
            dst_ref=place_of,
            send_sem=cots_send.at[way, chunk, shard],
            recv_sem=cots_recv.at[chunk, shard],
            device_id={"wide": to},
            device_id_type=MESH,
        )

    def outgoing(chunk, shard, climbs, drops, crosses):
        todo = []
        if climbs:
            todo.append((has_up, cots_copy(chunk, 0, shard, up)))
        if drops:
            todo.append((has_down, cots_copy(chunk, 1, shard, down)))
        if crosses:
            for at, other in enumerate(across):
                to = index_of(place, other, core)
                todo.append((None, cots_copy(chunk, 3 + at, shard, to)))
        todo.append((None, cots_copy(chunk, 2, shard, partner)))
        return todo

    def each(todo, act):
        for condition, copy in todo:
            if condition is None:
                act(copy)
            else:
                pl.when(condition)(functools.partial(act, copy))

    def start(copy):
        copy.start()

    def sent(copy):
        copy.wait_send()

    def arrived(chunk, shard):
        cots_copy(chunk, 2, shard, partner).wait_recv()

    def from_lines(chunk, step, act, wait):
        @pl.when(place - step >= 0)
        def _():
            shard = index_of(place - step, side, core)
            if wait:
                arrived(chunk, shard)
            each(outgoing(chunk, shard, True, False, True), act)

        @pl.when(place + step < lines)
        def _():
            shard = index_of(place + step, side, core)
            if wait:
                arrived(chunk, shard)
            each(outgoing(chunk, shard, False, True, True), act)

    def from_cross(chunk, step):
        for other in across:
            for sign in (1,) if step == 0 else (-1, 1):
                at = place + sign * step

                @pl.when((at >= 0) & (at < lines))
                def _():
                    shard = index_of(at, other, core)
                    arrived(chunk, shard)
                    each(outgoing(chunk, shard, False, False, False), start)

    def launch(chunk):
        own_cots(chunk).wait()
        each(outgoing(chunk, wide, True, True, True), start)

    def prepare():
        own_acts.wait()
        for off in range(1, n_narrow):
            acts_copy(off).wait()
        own_bits.wait()
        tile = 256
        offset = 0
        for seg, (low, high) in enumerate(windows):

            def one(at, _):
                begin = pl.multiple_of(low + at * tile, tile)
                values = acts_all[pl.ds(begin, tile), :].astype(jnp.float32)
                where_at = begin + lax.broadcasted_iota(jnp.int32, values.shape, 0)
                inside = (where_at >= bounds[0, seg]) & (where_at < bounds[1, seg])
                values = jnp.where(inside, values, 0.0)
                spot = pl.multiple_of(offset + at * tile, tile)
                flipped[:, pl.ds(spot, tile)] = values.T.astype(jnp.bfloat16)
                return 0

            lax.fori_loop(0, (high - low) // tile, one, 0)
            offset += high - low

    def compute(chunk):
        for at in range(lines):
            for over in range(cross):
                arrived(chunk, index_of(at, over, 1 - core))

        columns = columns_of(chunk)
        offset = 0
        for seg, (low, high) in enumerate(windows):
            grads[seg] = jnp.dot(
                flipped[:, offset : offset + high - low],
                bufs[chunk, low:high, :],
                preferred_element_type=jnp.float32,
            )
            offset += high - low
        for seg in range(seg_count):
            sign = (1 - 2 * bits_ref[:, columns]).astype(jnp.float32)
            grad = grads[seg] * (sign * gains[seg])
            parts = [
                grad[group * row_block : (group + 1) * row_block]
                for group in range(row_groups)
            ]
            for group, part in enumerate(butterflies(parts)):
                upper, lower = halves(part)
                mixed = jnp.dot(
                    left_ref[...], upper, preferred_element_type=jnp.float32
                ) + jnp.dot(left_ref[...], lower, preferred_element_type=jnp.float32)
                upper, lower = halves(mixed)
                mixed = jnp.dot(
                    upper, right_ref[...], preferred_element_type=jnp.float32
                ) + jnp.dot(lower, right_ref[...], preferred_element_type=jnp.float32)
                for lane_block in range(per_group):
                    block = chunk * per_group + lane_block
                    base = (block * rows + group * row_block) * seg_count + seg
                    table[pl.ds(base, row_block, stride=seg_count), :] = mixed[
                        :, lane_block * LANES : (lane_block + 1) * LANES
                    ]
        put_out(chunk).start()

    launch(0)
    for off in range(1, n_narrow):
        acts_copy(off).start()

    def slot_work(slot, _):
        @pl.when(slot + 1 < n_chunks)
        def _():
            launch(slot + 1)

        for step in range(lines, 0, -1):
            chunk = slot + 1 - step

            @pl.when((chunk >= 0) & (chunk < n_chunks))
            def _():
                if step < lines:
                    from_lines(chunk, step, start, True)
                from_cross(chunk, step - 1)

        pl.when(slot == lines)(prepare)

        @pl.when(slot >= lines)
        def _():
            compute(slot - lines)

        return 0

    lax.fori_loop(0, n_chunks + lines, slot_work, 0)

    def finish(chunk, _):
        each(outgoing(chunk, wide, True, True, True), sent)
        for step in range(1, lines):
            from_lines(chunk, step, sent, False)
        for at in range(lines):
            for other in across:
                shard = index_of(at, other, core)
                each(outgoing(chunk, shard, False, False, False), sent)
        put_out(chunk).wait()
        return 0

    lax.fori_loop(0, n_chunks, finish, 0)


def pick_kernel(seg_count, n_chunks, spots, parts_ref, signs_ref, out_ref, table):
    stretch = parts_ref.shape[0] // n_chunks

    def join(at, _):
        base = pl.multiple_of(at * 8, 8)
        spans = [pl.ds(base + chunk * stretch, 8) for chunk in range(n_chunks)]
        parts = butterflies([parts_ref[span, :] for span in spans])
        for span, part in zip(spans, parts):
            table[span, :] = part
        return 0

    lax.fori_loop(0, stretch // 8, join, 0, unroll=2)

    lane = lax.broadcasted_iota(jnp.int32, (8, LANES), 1)
    chains = 4

    def pick(group, _):
        found = [jnp.zeros((8, LANES), jnp.float32)] * chains
        for at in range(LANES):
            spot = spots[group * LANES + at]
            values = table[pl.ds(lax.shift_right_logical(spot, 7), 8), :]
            values = pltpu.roll(values, spot & (LANES - 1), 1)
            found[at % chains] = jnp.where(lane == at, values, found[at % chains])
        both = (found[0] + found[1]) + (found[2] + found[3])
        out_ref[group] = both[:seg_count] * signs_ref[pl.ds(group, 1), :]
        return 0

    lax.fori_loop(0, out_ref.shape[0], pick, 0)


def local_sketch(acts, cots, bits, lengths, spots, signs, n_wide, n_narrow):
    tokens = acts.shape[0] * n_narrow
    rows, cols = bits.shape
    seg_count = lengths.shape[0]
    groups = signs.shape[0]
    cross = 2
    row_block, col_block = min(rows, 256), min(cols, 256)
    n_chunks = cols // col_block
    windows = []
    for seg in range(seg_count):
        low = max(0, tokens - (seg_count - seg) * MOST) // 256 * 256
        high = min(tokens, -(-(seg + 1) * MOST // 256) * 256)
        windows.append((low, high))
    before = np.tril(np.ones((seg_count, seg_count), np.bool_))
    ends = jnp.sum(jnp.where(before, lengths[None, :], 0), axis=1)
    bounds = jnp.stack([ends - lengths, ends]).astype(jnp.int32)
    gains = lax.rsqrt(lengths.astype(jnp.float32))
    anywhere = pl.BlockSpec(memory_space=pl.ANY)
    scalars = pl.BlockSpec(memory_space=pltpu.SMEM)
    vectors = pl.BlockSpec(memory_space=pltpu.VMEM)
    table = rows * cols // LANES * seg_count
    parts = pl.pallas_call(
        functools.partial(sketch_kernel, n_wide, n_narrow, cross, tuple(windows), n_chunks),
        out_shape=jax.ShapeDtypeStruct((table, LANES), jnp.float32),
        in_specs=[scalars] * 2 + [anywhere] * 3 + [vectors] * 2,
        out_specs=anywhere,
        scratch_shapes=[
            pltpu.VMEM((tokens, rows), acts.dtype),
            pltpu.VMEM((rows, cols), bits.dtype),
            pltpu.VMEM((rows, sum(high - low for low, high in windows)), jnp.bfloat16),
            pltpu.VMEM((table, LANES), jnp.float32),
            pltpu.VMEM((n_chunks, cots.shape[0] * n_wide, col_block), cots.dtype),
            pltpu.VMEM((seg_count, rows, col_block), jnp.float32),
            pltpu.SemaphoreType.DMA((2 + 2 * n_chunks,)),
            pltpu.SemaphoreType.DMA((n_narrow,)),
            pltpu.SemaphoreType.DMA((n_narrow,)),
            pltpu.SemaphoreType.DMA((2 + cross, n_chunks, n_wide)),
            pltpu.SemaphoreType.DMA((n_chunks, n_wide)),
        ],
        compiler_params=pltpu.CompilerParams(
            collective_id=0, has_side_effects=True, vmem_limit_bytes=62 * 1024 * 1024
        ),
        name="local_sketch",
    )(bounds, gains, acts, cots, bits, sylvester(row_block), sylvester(col_block))
    return pl.pallas_call(
        functools.partial(pick_kernel, seg_count, n_chunks),
        out_shape=jax.ShapeDtypeStruct((groups, seg_count, LANES), jnp.float32),
        in_specs=[scalars, vectors, vectors],
        out_specs=vectors,
        scratch_shapes=[pltpu.VMEM((table + 8, LANES), jnp.float32)],
        compiler_params=pltpu.CompilerParams(vmem_limit_bytes=62 * 1024 * 1024),
        name="pick",
    )(spots, parts, signs)


def add_up_kernel(n_wide, n_narrow, shares, out, held, send_sem, recv_sem):
    count = n_wide * n_narrow
    me = lax.axis_index("wide") * n_narrow + lax.axis_index("narrow")
    barrier = pltpu.get_barrier_semaphore()

    def address(who):
        return {"wide": who // n_narrow, "narrow": lax.rem(who, n_narrow)}

    def greet(off, _):
        who = lax.rem(me + off, count)
        pl.semaphore_signal(barrier, inc=1, device_id=address(who), device_id_type=MESH)
        return 0

    lax.fori_loop(1, count, greet, 0)
    pl.semaphore_wait(barrier, count - 1)

    def copy_to(who, slot):
        return pltpu.make_async_remote_copy(
            src_ref=shares.at[who],
            dst_ref=held.at[slot],
            send_sem=send_sem.at[who],
            recv_sem=recv_sem.at[slot],
            device_id=address(who),
            device_id_type=MESH,
        )

    def send(off, _):
        copy_to(lax.rem(me + off, count), me).start()
        return 0

    lax.fori_loop(1, count, send, 0)
    out[...] = shares[me]

    def take(off, _):
        who = lax.rem(me + count - off, count)
        copy_to(who, who).wait_recv()
        out[...] += held[who]
        return 0

    lax.fori_loop(1, count, take, 0)

    def sent(off, _):
        copy_to(lax.rem(me + off, count), me).wait_send()
        return 0

    lax.fori_loop(1, count, sent, 0)


def add_up(shares, n_wide, n_narrow):
    count = n_wide * n_narrow
    in_vmem = pl.BlockSpec(memory_space=pltpu.VMEM)
    return pl.pallas_call(
        functools.partial(add_up_kernel, n_wide, n_narrow),
        out_shape=jax.ShapeDtypeStruct(shares.shape[1:], shares.dtype),
        in_specs=[in_vmem],
        out_specs=in_vmem,
        scratch_shapes=[
            pltpu.VMEM(shares.shape, shares.dtype),
            pltpu.SemaphoreType.DMA((count,)),
            pltpu.SemaphoreType.DMA((count,)),
        ],
        compiler_params=pltpu.CompilerParams(collective_id=1, has_side_effects=True),
        name="add_up",
    )(shares)


def body(n_wide, n_narrow, activations, cotangent, sign_bits, seg_lengths, kept_index):
    rows, cols = sign_bits.shape
    seg_count = seg_lengths.shape[0]
    kept = kept_index.shape[0]
    count = n_wide * n_narrow
    scale = 1.0 / math.sqrt(rows * n_wide * cols * n_narrow)
    full_cols = cols * n_narrow
    row_of = kept_index // full_cols
    col_of = kept_index % full_cols
    common = lax.population_count((row_of // rows) & lax.axis_index("wide"))
    common = common + lax.population_count((col_of // cols) & lax.axis_index("narrow"))
    signs = (1 - 2 * (common & 1)).astype(jnp.float32) * scale
    col = col_of % cols
    row = ((col // LANES) * rows + row_of % rows) * seg_count
    lane = jnp.arange(kept, dtype=jnp.int32)
    spots = row * LANES + ((lane - col) & (LANES - 1))
    shares = local_sketch(
        activations, cotangent, sign_bits, seg_lengths, spots, signs.reshape(-1, LANES),
        n_wide, n_narrow,
    )
    each = kept // count
    if each % LANES:
        flat = shares.transpose(1, 0, 2).reshape(seg_count, kept)
        return lax.psum_scatter(flat, ("wide", "narrow"), scatter_dimension=1, tiled=True)
    mine = add_up(shares.reshape(count, -1, LANES), n_wide, n_narrow)
    mine = mine.reshape(each // LANES, seg_count, LANES)
    return mine.transpose(1, 0, 2).reshape(seg_count, each)


def solution(mesh):
    return jax.shard_map(
        functools.partial(body, mesh.shape["wide"], mesh.shape["narrow"]),
        mesh=mesh,
        in_specs=(P("narrow", "wide"), P("wide", "narrow"), P("wide", "narrow"), P(), P()),
        out_specs=P(None, ("wide", "narrow")),
        check_vma=False,
    )
```

```python
import functools
import math

import jax
import jax.numpy as jnp
from jax import lax
from jax.experimental import pallas as pl
from jax.experimental.pallas import tpu as pltpu
from jax.sharding import PartitionSpec as P

LANES = 128
HALF = LANES // 2
MOST = 1536
TILE = 256
PAD = 8
MESH = pl.DeviceIdType.MESH


def parity(values):
    for shift in (16, 8, 4, 2, 1):
        values = values ^ lax.shift_right_logical(values, shift)
    return values & 1


def sylvester(extent):
    rows = lax.broadcasted_iota(jnp.int32, (extent, extent), 0)
    cols = lax.broadcasted_iota(jnp.int32, (extent, extent), 1)
    return (1 - 2 * parity(rows & cols)).astype(jnp.float32).astype(jnp.bfloat16)


def butterflies(parts):
    parts = list(parts)
    gap = 1
    while gap < len(parts):
        for low in range(len(parts)):
            if not low & gap:
                one, two = parts[low], parts[low | gap]
                parts[low], parts[low | gap] = one + two, one - two
        gap *= 2
    return parts


def halves(values):
    high = values.astype(jnp.bfloat16)
    low = (values - high.astype(jnp.float32)).astype(jnp.bfloat16)
    return high, low


def log2(extent):
    return extent.bit_length() - 1


def sketch_kernel(
    n_wide, n_narrow, cross, windows, n_chunks, scatter, full_shape,
    lengths, kept, acts, cots, bits_in,
    out_ref, acts_all, bits_ref, flipped, table, bufs, grads, left_ref, right_ref,
    rows_at, lanes_at, signs_at, spots, shares, held,
    local_sem, spots_sem, acts_send, acts_recv, cots_send, cots_recv, share_send, share_recv,
):
    wide = lax.axis_index("wide")
    narrow = lax.axis_index("narrow")
    count = n_wide * n_narrow
    me = wide * n_narrow + narrow
    lines = n_wide // (2 * cross)
    core = lax.rem(wide, 2)
    side = lax.rem(wide // 2, cross)
    place = wide // (2 * cross)
    mate = place + 1 - 2 * lax.rem(place, 2)
    tok_acts = acts.shape[0]
    tok_cots = cots.shape[0]
    tokens = acts_all.shape[0]
    rows, cols = bits_in.shape
    row_block = left_ref.shape[0]
    col_block = right_ref.shape[0]
    row_groups = rows // row_block
    per_group = col_block // LANES
    seg_count = len(windows)
    stretch = per_group * rows * seg_count
    blocks, per_block = kept.shape[:2]
    pieces = acts_send.shape[1]
    piece = tok_acts // pieces

    def index_of(at, across, on_core):
        return (at * cross + across) * 2 + on_core

    partner = index_of(place, side, 1 - core)
    up = index_of(lax.rem(place + 1, lines), side, core)
    down = index_of(lax.rem(place + lines - 1, lines), side, core)
    other_side = 1 - side
    over = index_of(place, other_side, core)
    mate_index = index_of(mate, side, core)
    has_up = place < lines - 1
    has_down = place > 0

    my_cots = pl.ds(wide * tok_cots, tok_cots)

    def columns_of(chunk):
        return pl.ds(pl.multiple_of(chunk * col_block, col_block), col_block)

    def own_cots(chunk):
        return pltpu.make_async_copy(
            cots.at[:, columns_of(chunk)], bufs.at[chunk, my_cots, :], local_sem.at[2 + chunk]
        )

    own_acts = pltpu.make_async_copy(
        acts, acts_all.at[pl.ds(narrow * tok_acts, tok_acts), :], local_sem.at[0]
    )
    own_bits = pltpu.make_async_copy(bits_in, bits_ref, local_sem.at[1])
    for chunk in range(n_chunks):
        own_cots(chunk).start()
    own_acts.start()
    own_bits.start()

    barrier = pltpu.get_barrier_semaphore()

    def address(who):
        return {"wide": who // n_narrow, "narrow": lax.rem(who, n_narrow)}

    def greet(off, _):
        who = lax.rem(me + off, count)
        pl.semaphore_signal(barrier, inc=1, device_id=address(who), device_id_type=MESH)
        return 0

    lax.fori_loop(1, count, greet, 0)
    pl.semaphore_wait(barrier, count - 1)

    def acts_copy(off, part):
        spot = pl.multiple_of(part * piece, piece)
        return pltpu.make_async_remote_copy(
            src_ref=acts.at[pl.ds(spot, piece), :],
            dst_ref=acts_all.at[pl.ds(narrow * tok_acts + spot, piece), :],
            send_sem=acts_send.at[off, part],
            recv_sem=acts_recv.at[off, part],
            device_id={"narrow": lax.rem(narrow + off, n_narrow)},
            device_id_type=MESH,
        )

    def cots_copy(chunk, way, shard, to):
        place_of = bufs.at[chunk, pl.ds(shard * tok_cots, tok_cots), :]
        return pltpu.make_async_remote_copy(
            src_ref=place_of,
            dst_ref=place_of,
            send_sem=cots_send.at[way, chunk, shard],
            recv_sem=cots_recv.at[chunk, shard],
            device_id={"wide": to},
            device_id_type=MESH,
        )

    def turn(chunk):
        return core == lax.rem(chunk, 2)

    def from_own_side(chunk, at, climbs, drops):
        shard = index_of(at, side, core)
        todo = [(~((at == mate) & turn(chunk)), cots_copy(chunk, 3, shard, over))]
        if climbs:
            todo.append((has_up, cots_copy(chunk, 0, shard, up)))
        if drops:
            todo.append((has_down, cots_copy(chunk, 1, shard, down)))
        todo.append((None, cots_copy(chunk, 2, shard, partner)))
        return todo

    def from_other_side(chunk, at):
        shard = index_of(at, other_side, core)
        return [
            ((at == place) & turn(chunk), cots_copy(chunk, 0, shard, mate_index)),
            (None, cots_copy(chunk, 2, shard, partner)),
        ]

    def each(todo, act):
        for condition, copy in todo:
            if condition is None:
                act(copy)
            else:
                pl.when(condition)(functools.partial(act, copy))

    def start(copy):
        copy.start()

    def sent(copy):
        copy.wait_send()

    def arrived(chunk, shard):
        cots_copy(chunk, 2, shard, partner).wait_recv()

    def along(chunk, step, act, wait):
        @pl.when(place - step >= 0)
        def _():
            if wait:
                arrived(chunk, index_of(place - step, side, core))
            each(from_own_side(chunk, place - step, True, False), act)

        @pl.when(place + step < lines)
        def _():
            if wait:
                arrived(chunk, index_of(place + step, side, core))
            each(from_own_side(chunk, place + step, False, True), act)

    def across(chunk, step):
        for way in (1,) if step == 0 else (-1, 1):
            at = place + way * step

            @pl.when((at >= 0) & (at < lines))
            def _():
                arrived(chunk, index_of(at, other_side, core))
                each(from_other_side(chunk, at), start)

    def launch(chunk):
        own_cots(chunk).wait()
        each(from_own_side(chunk, place, True, True), start)

    starts = []
    total = 0
    for seg in range(seg_count):
        starts.append(total)
        total = total + lengths[seg]
    starts.append(total)

    def flip(begin):
        begin = pl.multiple_of(begin, TILE)
        values = acts_all[pl.ds(begin, TILE), :].astype(jnp.float32).T
        where_at = begin + lax.broadcasted_iota(jnp.int32, values.shape, 1)
        offset = 0
        for seg, (low, high) in enumerate(windows):

            @pl.when((begin >= low) & (begin < high))
            def _():
                inside = (where_at >= starts[seg]) & (where_at < starts[seg + 1])
                spot = pl.multiple_of(offset + begin - low, TILE)
                flipped[:, pl.ds(spot, TILE)] = jnp.where(inside, values, 0.0).astype(jnp.bfloat16)

            offset += high - low

    def flip_own(part, _):
        spot = narrow * tok_acts + part * piece

        def one(at, _):
            flip(spot + at * TILE)
            return 0

        return lax.fori_loop(0, piece // TILE, one, 0)

    def flip_far(part, _):
        for off in range(1, n_narrow):
            acts_copy(off, part).wait_recv()
            spot = lax.rem(narrow + n_narrow - off, n_narrow) * tok_acts + part * piece

            def one(at, _):
                flip(spot + at * TILE)
                return 0

            lax.fori_loop(0, piece // TILE, one, 0)
        return 0

    def prologue():
        left_ref[...] = sylvester(row_block)
        right_ref[...] = sylvester(col_block)
        table[pl.ds(0, PAD), :] = jnp.zeros((PAD, LANES), jnp.float32)
        table[pl.ds(PAD + n_chunks * stretch, PAD), :] = jnp.zeros((PAD, LANES), jnp.float32)
        full_rows, full_cols = full_shape
        scale = 1.0 / math.sqrt(full_rows * full_cols)
        index = kept[...]
        row_of = lax.shift_right_logical(index, log2(full_cols))
        col_of = index & (full_cols - 1)
        common = lax.shift_right_logical(row_of, log2(rows)) & wide
        odd = parity(common) ^ parity(lax.shift_right_logical(col_of, log2(cols)) & narrow)
        signs_at[...] = (1 - 2 * odd).astype(jnp.float32) * scale
        col = col_of & (cols - 1)
        lane_block = lax.shift_right_logical(col, log2(LANES))
        rows_at[...] = (lane_block * rows + (row_of & (rows - 1))) * seg_count
        lanes_at[...] = col & (LANES - 1)

    def compute(chunk, _):
        for at in range(lines):
            for off in range(cross):
                arrived(chunk, index_of(at, off, 1 - core))

        columns = columns_of(chunk)
        offset = 0
        for seg, (low, high) in enumerate(windows):
            grads[seg] = jnp.dot(
                flipped[:, offset : offset + high - low],
                bufs[chunk, low:high, :],
                preferred_element_type=jnp.float32,
            )
            offset += high - low
        for seg in range(seg_count):
            gain = lax.rsqrt(jnp.full((1, col_block), lengths[seg], jnp.int32).astype(jnp.float32))
            sign = (1 - 2 * bits_ref[:, columns]).astype(jnp.float32)
            grad = grads[seg] * (sign * gain)
            parts = [
                grad[group * row_block : (group + 1) * row_block]
                for group in range(row_groups)
            ]
            for group, part in enumerate(butterflies(parts)):
                upper, lower = halves(part)
                mixed = jnp.dot(
                    left_ref[...], upper, preferred_element_type=jnp.float32
                ) + jnp.dot(left_ref[...], lower, preferred_element_type=jnp.float32)
                upper, lower = halves(mixed)
                mixed = jnp.dot(
                    upper, right_ref[...], preferred_element_type=jnp.float32
                ) + jnp.dot(lower, right_ref[...], preferred_element_type=jnp.float32)
                for lane_block in range(per_group):
                    block = chunk * per_group + lane_block
                    base = PAD + (block * rows + group * row_block) * seg_count + seg
                    table[pl.ds(base, row_block, stride=seg_count), :] = mixed[
                        :, lane_block * LANES : (lane_block + 1) * LANES
                    ]
        return 0

    launch(0)
    for part in range(pieces):
        for off in range(1, n_narrow):
            acts_copy(off, part).start()

    lag = lines + 1

    def slot_work(slot, _):
        @pl.when(slot + 1 < n_chunks)
        def _():
            launch(slot + 1)

        for step in range(lines, 0, -1):
            chunk = slot + 1 - step

            @pl.when((chunk >= 0) & (chunk < n_chunks))
            def _():
                if step < lines:
                    along(chunk, step, start, True)
                across(chunk, step - 1)

        @pl.when(slot == 0)
        def _():
            prologue()
            own_acts.wait()

        near = lax.clamp(0, slot, pieces)
        lax.fori_loop(near, lax.clamp(0, slot + 1, pieces), flip_own, 0)
        far_from = lax.clamp(0, slot - 2, pieces)
        far_to = jnp.where(slot >= lag, pieces, lax.clamp(0, slot - 1, pieces))
        lax.fori_loop(jnp.where(slot > lag, pieces, far_from), far_to, flip_far, 0)
        pl.when(slot == lag)(own_bits.wait)

        def done(at):
            ready = lax.clamp(0, at - lines + 1, n_chunks)
            return jnp.where(at < lag, 0, ready)

        lax.fori_loop(done(slot - 1), done(slot), compute, 0)
        return 0

    lax.fori_loop(0, max(n_chunks + lines, lag + 1), slot_work, 0)

    def fetch(block, half):
        return pltpu.make_async_copy(rows_at.at[block], spots.at[half], spots_sem.at[half])

    def block_at(turn_at):
        return lax.rem(me + turn_at + 1, count) if scatter else turn_at

    for half in range(2):
        fetch(block_at(half), half).start()

    def join(at, _):
        base = pl.multiple_of(PAD + at * 8, 8)
        spans = [pl.ds(base + chunk * stretch, 8) for chunk in range(n_chunks)]
        parts = butterflies([table[span, :] for span in spans])
        for span, part in zip(spans, parts):
            table[span, :] = part
        return 0

    lax.fori_loop(0, stretch // 8, join, 0, unroll=4)

    lane = lax.broadcasted_iota(jnp.int32, (8, LANES), 1)
    row = lax.broadcasted_iota(jnp.int32, (8, LANES), 0)
    first = row < seg_count
    place_in = lane & (HALF - 1)

    def share_copy(who, slot):
        return pltpu.make_async_remote_copy(
            src_ref=shares.at[who],
            dst_ref=held.at[slot],
            send_sem=share_send.at[who],
            recv_sem=share_recv.at[slot],
            device_id=address(who),
            device_id_type=MESH,
        )

    def pick(pair, _):
        for half in range(2):
            turn_at = pair * 2 + half
            block = block_at(turn_at)
            fetch(block, half).wait()
            for group in range(per_block):
                lanes = jnp.broadcast_to(lanes_at[block, group : group + 1, :], (8, LANES))
                found = [jnp.zeros((8, LANES), jnp.float32)] * 2
                for at in range(HALF):
                    one = spots[half, group, at]
                    two = spots[half, group, at + HALF]
                    values = jnp.where(
                        first, table[pl.ds(one + PAD, 8), :], table[pl.ds(two + PAD - seg_count, 8), :]
                    )
                    values = jnp.take_along_axis(values, lanes, axis=1)
                    found[at % 2] = jnp.where(place_in == at, values, found[at % 2])
                both = found[0] + found[1]
                picked = jnp.where(
                    lane[:seg_count] < HALF, both[:seg_count], both[seg_count : 2 * seg_count]
                )
                shares[block, group * seg_count : (group + 1) * seg_count, :] = (
                    picked * signs_at[block, group : group + 1, :]
                )

            @pl.when(turn_at + 2 < blocks)
            def _():
                fetch(block_at(turn_at + 2), half).start()

            if scatter:

                @pl.when(turn_at + 1 < count)
                def _():
                    share_copy(block, me).start()
        return 0

    lax.fori_loop(0, blocks // 2, pick, 0)

    if scatter:

        def take(off, total):
            who = lax.rem(me + count - off, count)
            share_copy(who, who).wait_recv()
            return total + held[who]

        total = lax.fori_loop(1, count, take, shares[me])
        for group in range(per_block):
            out_ref[:, group * LANES : (group + 1) * LANES] = total[
                group * seg_count : (group + 1) * seg_count
            ]

        def gone(off, _):
            share_copy(lax.rem(me + off, count), me).wait_send()
            return 0

        lax.fori_loop(1, count, gone, 0)
    else:
        out_ref[...] = shares[...]

    def finish(chunk, _):
        each(from_own_side(chunk, place, True, True), sent)
        for step in range(1, lines):
            along(chunk, step, sent, False)
        for at in range(lines):
            each(from_other_side(chunk, at), sent)
        return 0

    lax.fori_loop(0, n_chunks, finish, 0)
    for part in range(pieces):
        for off in range(1, n_narrow):
            acts_copy(off, part).wait_send()


def body(n_wide, n_narrow, activations, cotangent, sign_bits, seg_lengths, kept_index):
    tokens = activations.shape[0] * n_narrow
    rows, cols = sign_bits.shape
    seg_count = seg_lengths.shape[0]
    kept = kept_index.shape[0]
    count = n_wide * n_narrow
    each = kept // count
    scatter = each % LANES == 0
    per_block = each // LANES if scatter else 4
    blocks = kept // LANES // per_block
    cross = 2
    row_block, col_block = min(rows, 256), min(cols, 256)
    n_chunks = cols // col_block
    windows = []
    for seg in range(seg_count):
        low = max(0, tokens - (seg_count - seg) * MOST) // TILE * TILE
        high = min(tokens, -(-(seg + 1) * MOST // TILE) * TILE)
        windows.append((low, high))
    pieces = max(1, activations.shape[0] // 512)
    anywhere = pl.BlockSpec(memory_space=pl.ANY)
    scalars = pl.BlockSpec(memory_space=pltpu.SMEM)
    vectors = pl.BlockSpec(memory_space=pltpu.VMEM)
    table = rows * cols // LANES * seg_count + 2 * PAD
    block_shape = (blocks, per_block, LANES)
    share_shape = (blocks, per_block * seg_count, LANES)
    out = (seg_count, each) if scatter else share_shape
    shares = pl.pallas_call(
        functools.partial(
            sketch_kernel, n_wide, n_narrow, cross, tuple(windows), n_chunks, scatter,
            (rows * n_wide, cols * n_narrow),
        ),
        out_shape=jax.ShapeDtypeStruct(out, jnp.float32),
        in_specs=[scalars, vectors] + [anywhere] * 3,
        out_specs=vectors,
        scratch_shapes=[
            pltpu.VMEM((tokens, rows), activations.dtype),
            pltpu.VMEM((rows, cols), sign_bits.dtype),
            pltpu.VMEM((rows, sum(high - low for low, high in windows)), jnp.bfloat16),
            pltpu.VMEM((table, LANES), jnp.float32),
            pltpu.VMEM((n_chunks, cotangent.shape[0] * n_wide, col_block), cotangent.dtype),
            pltpu.VMEM((seg_count, rows, col_block), jnp.float32),
            pltpu.VMEM((row_block, row_block), jnp.bfloat16),
            pltpu.VMEM((col_block, col_block), jnp.bfloat16),
            pltpu.VMEM(block_shape, jnp.int32),
            pltpu.VMEM(block_shape, jnp.int32),
            pltpu.VMEM(block_shape, jnp.float32),
            pltpu.SMEM((2, per_block, LANES), jnp.int32),
            pltpu.VMEM(share_shape, jnp.float32),
            pltpu.VMEM(share_shape, jnp.float32),
            pltpu.SemaphoreType.DMA((2 + n_chunks,)),
            pltpu.SemaphoreType.DMA((2,)),
            pltpu.SemaphoreType.DMA((n_narrow, pieces)),
            pltpu.SemaphoreType.DMA((n_narrow, pieces)),
            pltpu.SemaphoreType.DMA((4, n_chunks, n_wide)),
            pltpu.SemaphoreType.DMA((n_chunks, n_wide)),
            pltpu.SemaphoreType.DMA((blocks,)),
            pltpu.SemaphoreType.DMA((blocks,)),
        ],
        compiler_params=pltpu.CompilerParams(
            collective_id=0, has_side_effects=True, vmem_limit_bytes=62 * 1024 * 1024
        ),
        name="sketch",
    )(seg_lengths, kept_index.reshape(block_shape), activations, cotangent, sign_bits)
    if scatter:
        return shares
    flat = shares.reshape(blocks, per_block, seg_count, LANES)
    flat = flat.transpose(2, 0, 1, 3).reshape(seg_count, kept)
    return lax.psum_scatter(flat, ("wide", "narrow"), scatter_dimension=1, tiled=True)


def solution(mesh):
    return jax.shard_map(
        functools.partial(body, mesh.shape["wide"], mesh.shape["narrow"]),
        mesh=mesh,
        in_specs=(P("narrow", "wide"), P("wide", "narrow"), P("wide", "narrow"), P(), P()),
        out_specs=P(None, ("wide", "narrow")),
        check_vma=False,
    )
```

```python
import functools
import math

import jax
import jax.numpy as jnp
from jax import lax
from jax.experimental import pallas as pl
from jax.experimental.pallas import tpu as pltpu
from jax.sharding import PartitionSpec as P

LANES = 128
HALF = LANES // 2
MOST = 1536
TILE = 256
PAD = 8
MESH = pl.DeviceIdType.MESH


def parity(values):
    for shift in (16, 8, 4, 2, 1):
        values = values ^ lax.shift_right_logical(values, shift)
    return values & 1


def sylvester(extent):
    rows = lax.broadcasted_iota(jnp.int32, (extent, extent), 0)
    cols = lax.broadcasted_iota(jnp.int32, (extent, extent), 1)
    return (1 - 2 * parity(rows & cols)).astype(jnp.float32).astype(jnp.bfloat16)


def butterflies(parts):
    parts = list(parts)
    gap = 1
    while gap < len(parts):
        for low in range(len(parts)):
            if not low & gap:
                one, two = parts[low], parts[low | gap]
                parts[low], parts[low | gap] = one + two, one - two
        gap *= 2
    return parts


def halves(values):
    high = values.astype(jnp.bfloat16)
    low = (values - high.astype(jnp.float32)).astype(jnp.bfloat16)
    return high, low


def log2(extent):
    return extent.bit_length() - 1


def sketch_kernel(
    n_wide, n_narrow, cross, windows, n_chunks, scatter, full_shape,
    lengths, kept, acts, cots, bits_in,
    out_ref, acts_all, bits_ref, flipped, table, bufs, grads, left_ref, right_ref,
    rows_at, lanes_at, signs_at, spots, shares, held,
    local_sem, spots_sem, acts_send, acts_recv, cots_send, mate_send, cots_recv, both_recv,
    share_send, share_recv,
):
    wide = lax.axis_index("wide")
    narrow = lax.axis_index("narrow")
    count = n_wide * n_narrow
    me = wide * n_narrow + narrow
    lines = n_wide // (2 * cross)
    core = lax.rem(wide, 2)
    side = lax.rem(wide // 2, cross)
    place = wide // (2 * cross)
    mate = place + 1 - 2 * lax.rem(place, 2)
    tok_acts = acts.shape[0]
    tok_cots = cots.shape[0]
    tokens = acts_all.shape[0]
    rows, cols = bits_in.shape
    row_block = left_ref.shape[0]
    col_block = right_ref.shape[0]
    row_groups = rows // row_block
    per_group = col_block // LANES
    seg_count = len(windows)
    stretch = per_group * rows * seg_count
    blocks, per_block = kept.shape[:2]
    pieces = acts_send.shape[1]
    piece = tok_acts // pieces

    def index_of(at, across, on_core):
        return (at * cross + across) * 2 + on_core

    partner = index_of(place, side, 1 - core)
    up = index_of(lax.rem(place + 1, lines), side, core)
    down = index_of(lax.rem(place + lines - 1, lines), side, core)
    other_side = 1 - side
    over = index_of(place, other_side, core)
    mate_index = index_of(mate, side, core)
    has_up = place < lines - 1
    has_down = place > 0

    my_cots = pl.ds(wide * tok_cots, tok_cots)

    def columns_of(chunk):
        return pl.ds(pl.multiple_of(chunk * col_block, col_block), col_block)

    def own_cots(chunk):
        return pltpu.make_async_copy(
            cots.at[:, columns_of(chunk)], bufs.at[chunk, my_cots, :], local_sem.at[2]
        )

    own_acts = pltpu.make_async_copy(
        acts, acts_all.at[pl.ds(narrow * tok_acts, tok_acts), :], local_sem.at[0]
    )
    own_bits = pltpu.make_async_copy(bits_in, bits_ref, local_sem.at[1])
    for chunk in range(n_chunks):
        own_cots(chunk).start()
    own_acts.start()
    own_bits.start()

    barrier = pltpu.get_barrier_semaphore()

    def address(who):
        return {"wide": who // n_narrow, "narrow": lax.rem(who, n_narrow)}

    def greet(off, _):
        who = lax.rem(me + off, count)
        pl.semaphore_signal(barrier, inc=1, device_id=address(who), device_id_type=MESH)
        return 0

    lax.fori_loop(1, count, greet, 0)
    pl.semaphore_wait(barrier, count - 1)

    def acts_copy(off, part):
        spot = pl.multiple_of(part * piece, piece)
        return pltpu.make_async_remote_copy(
            src_ref=acts.at[pl.ds(spot, piece), :],
            dst_ref=acts_all.at[pl.ds(narrow * tok_acts + spot, piece), :],
            send_sem=acts_send.at[off - 1, part],
            recv_sem=acts_recv.at[off - 1, part],
            device_id={"narrow": lax.rem(narrow + off, n_narrow)},
            device_id_type=MESH,
        )

    def cots_copy(chunk, shard, to, send_sem, own=False):
        place_of = bufs.at[chunk, pl.ds(shard * tok_cots, tok_cots), :]
        return pltpu.make_async_remote_copy(
            src_ref=cots.at[:, columns_of(chunk)] if own else place_of,
            dst_ref=place_of,
            send_sem=send_sem,
            recv_sem=both_recv.at[chunk] if to is partner else cots_recv.at[chunk, shard // 2],
            device_id={"wide": to},
            device_id_type=MESH,
        )

    def turn(chunk):
        return core == lax.rem(chunk, 2)

    def from_own_side(chunk, at, climbs, drops, own=False):
        shard = index_of(at, side, core)
        step = lax.rem(chunk, 2)

        def to_device(way, to):
            return cots_copy(chunk, shard, to, cots_send.at[way, step, at], own)

        todo = [(~((at == mate) & turn(chunk)), to_device(3, over))]
        if climbs:
            todo.append((has_up, to_device(0, up)))
        if drops:
            todo.append((has_down, to_device(1, down)))
        todo.append((None, to_device(2, partner)))
        return todo

    def from_other_side(chunk, at):
        shard = index_of(at, other_side, core)
        step = lax.rem(chunk, 2)
        return [
            ((at == place) & turn(chunk), cots_copy(chunk, shard, mate_index, mate_send.at[step])),
            (None, cots_copy(chunk, shard, partner, cots_send.at[4, step, at])),
        ]

    def each(todo, act):
        for condition, copy in todo:
            if condition is None:
                act(copy)
            else:
                pl.when(condition)(functools.partial(act, copy))

    def sent(copy):
        copy.wait_send()

    def start(chunk, todo):
        for condition, copy in todo:

            def act():
                pl.when(chunk >= 2)(copy.wait_send)
                copy.start()

            if condition is None:
                act()
            else:
                pl.when(condition)(act)

    def arrived(chunk, shard):
        cots_copy(chunk, shard, up, mate_send.at[0]).wait_recv()

    def along(chunk, step, act, wait):
        @pl.when(place - step >= 0)
        def _():
            if wait:
                arrived(chunk, index_of(place - step, side, core))
            act(from_own_side(chunk, place - step, True, False))

        @pl.when(place + step < lines)
        def _():
            if wait:
                arrived(chunk, index_of(place + step, side, core))
            act(from_own_side(chunk, place + step, False, True))

    def across(chunk, step):
        for way in (1,) if step == 0 else (-1, 1):
            at = place + way * step

            @pl.when((at >= 0) & (at < lines))
            def _():
                arrived(chunk, index_of(at, other_side, core))
                start(chunk, from_other_side(chunk, at))

    def launch(chunk):
        start(chunk, from_own_side(chunk, place, True, True, True))

    starts = []
    total = 0
    for seg in range(seg_count):
        starts.append(total)
        total = total + lengths[seg]
    starts.append(total)

    def flip(begin):
        begin = pl.multiple_of(begin, TILE)
        values = acts_all[pl.ds(begin, TILE), :].astype(jnp.float32).T
        where_at = begin + lax.broadcasted_iota(jnp.int32, values.shape, 1)
        offset = 0
        for seg, (low, high) in enumerate(windows):

            @pl.when((begin >= low) & (begin < high))
            def _():
                inside = (where_at >= starts[seg]) & (where_at < starts[seg + 1])
                spot = pl.multiple_of(offset + begin - low, TILE)
                flipped[:, pl.ds(spot, TILE)] = jnp.where(inside, values, 0.0).astype(jnp.bfloat16)

            offset += high - low

    def flip_own(part, _):
        spot = narrow * tok_acts + part * piece

        def one(at, _):
            flip(spot + at * TILE)
            return 0

        return lax.fori_loop(0, piece // TILE, one, 0)

    def flip_far(part, _):
        for off in range(1, n_narrow):
            acts_copy(off, part).wait_recv()
            spot = lax.rem(narrow + n_narrow - off, n_narrow) * tok_acts + part * piece

            def one(at, _):
                flip(spot + at * TILE)
                return 0

            lax.fori_loop(0, piece // TILE, one, 0)
        return 0

    def prologue():
        left_ref[...] = sylvester(row_block)
        right_ref[...] = sylvester(col_block)
        table[pl.ds(0, PAD), :] = jnp.zeros((PAD, LANES), jnp.float32)
        table[pl.ds(PAD + n_chunks * stretch, PAD), :] = jnp.zeros((PAD, LANES), jnp.float32)
        full_rows, full_cols = full_shape
        scale = 1.0 / math.sqrt(full_rows * full_cols)
        index = kept[...]
        row_of = lax.shift_right_logical(index, log2(full_cols))
        col_of = index & (full_cols - 1)
        common = lax.shift_right_logical(row_of, log2(rows)) & wide
        odd = parity(common) ^ parity(lax.shift_right_logical(col_of, log2(cols)) & narrow)
        signs_at[...] = (1 - 2 * odd).astype(jnp.float32) * scale
        col = col_of & (cols - 1)
        lane_block = lax.shift_right_logical(col, log2(LANES))
        rows_at[...] = (lane_block * rows + (row_of & (rows - 1))) * seg_count
        lanes_at[...] = col & (LANES - 1)

    def compute(chunk, _):
        half_rows = bufs.at[chunk, pl.ds(0, tokens // 2), :]
        pltpu.make_async_remote_copy(
            src_ref=half_rows,
            dst_ref=half_rows,
            send_sem=mate_send.at[0],
            recv_sem=both_recv.at[chunk],
            device_id={"wide": partner},
            device_id_type=MESH,
        ).wait_recv()

        columns = columns_of(chunk)
        offset = 0
        for seg, (low, high) in enumerate(windows):
            grads[seg] = jnp.dot(
                flipped[:, offset : offset + high - low],
                bufs[chunk, low:high, :],
                preferred_element_type=jnp.float32,
            )
            offset += high - low
        for seg in range(seg_count):
            gain = lax.rsqrt(jnp.full((1, col_block), lengths[seg], jnp.int32).astype(jnp.float32))
            sign = (1 - 2 * bits_ref[:, columns]).astype(jnp.float32)
            grad = grads[seg] * (sign * gain)
            parts = [
                grad[group * row_block : (group + 1) * row_block]
                for group in range(row_groups)
            ]
            for group, part in enumerate(butterflies(parts)):
                upper, lower = halves(part)
                mixed = jnp.dot(
                    left_ref[...], upper, preferred_element_type=jnp.float32
                ) + jnp.dot(left_ref[...], lower, preferred_element_type=jnp.float32)
                upper, lower = halves(mixed)
                mixed = jnp.dot(
                    upper, right_ref[...], preferred_element_type=jnp.float32
                ) + jnp.dot(lower, right_ref[...], preferred_element_type=jnp.float32)
                for lane_block in range(per_group):
                    block = chunk * per_group + lane_block
                    base = PAD + (block * rows + group * row_block) * seg_count + seg
                    table[pl.ds(base, row_block, stride=seg_count), :] = mixed[
                        :, lane_block * LANES : (lane_block + 1) * LANES
                    ]
        return 0

    launch(0)
    for part in range(pieces):
        for off in range(1, n_narrow):
            acts_copy(off, part).start()

    lag = lines + 1

    def slot_work(slot, _):
        @pl.when(slot + 1 < n_chunks)
        def _():
            launch(slot + 1)

        for step in range(lines - 1, 0, -1):
            chunk = slot + 1 - step

            @pl.when((chunk >= 0) & (chunk < n_chunks))
            def _():
                along(chunk, step, functools.partial(start, chunk), True)

        @pl.when(slot == 0)
        def _():
            prologue()
            own_acts.wait()

        lax.fori_loop(lax.clamp(0, slot, pieces), lax.clamp(0, slot + 1, pieces), flip_own, 0)

        for step in range(lines, 0, -1):
            chunk = slot + 1 - step

            @pl.when((chunk >= 0) & (chunk < n_chunks))
            def _():
                across(chunk, step - 1)

        far = slot - (lag - pieces)
        far_from = jnp.where(slot > lag, pieces, lax.clamp(0, far - 1, pieces))
        far_to = jnp.where(slot >= lag, pieces, lax.clamp(0, far, pieces))
        lax.fori_loop(far_from, far_to, flip_far, 0)

        @pl.when(slot == lag)
        def _():
            own_bits.wait()
            pltpu.make_async_copy(
                bufs.at[:, my_cots, :], bufs.at[:, my_cots, :], local_sem.at[2]
            ).wait()

        def done(at):
            ready = jnp.minimum(2 * (at - lag) + 1, at - lines + 2)
            ready = jnp.where(at >= last, n_chunks, ready)
            return jnp.where(at < lag, 0, lax.clamp(0, ready, n_chunks))

        lax.fori_loop(done(slot - 1), done(slot), compute, 0)
        return 0

    last = max(n_chunks + lines - 2, lag)
    lax.fori_loop(0, last + 1, slot_work, 0)

    def fetch(block, half):
        return pltpu.make_async_copy(rows_at.at[block], spots.at[half], spots_sem.at[half])

    def block_at(turn_at):
        return lax.rem(me + turn_at + 1, count) if scatter else turn_at

    for half in range(2):
        fetch(block_at(half), half).start()

    def join(at, _):
        base = pl.multiple_of(PAD + at * 8, 8)
        spans = [pl.ds(base + chunk * stretch, 8) for chunk in range(n_chunks)]
        parts = butterflies([table[span, :] for span in spans])
        for span, part in zip(spans, parts):
            table[span, :] = part
        return 0

    lax.fori_loop(0, stretch // 8, join, 0, unroll=4)

    lane = lax.broadcasted_iota(jnp.int32, (8, LANES), 1)
    row = lax.broadcasted_iota(jnp.int32, (8, LANES), 0)
    first = row < seg_count
    place_in = lane & (HALF - 1)

    def share_copy(who, slot):
        return pltpu.make_async_remote_copy(
            src_ref=shares.at[who],
            dst_ref=held.at[slot],
            send_sem=share_send,
            recv_sem=share_recv,
            device_id=address(who),
            device_id_type=MESH,
        )

    def pick(pair, _):
        for half in range(2):
            turn_at = pair * 2 + half
            block = block_at(turn_at)
            fetch(block, half).wait()
            for group in range(per_block):
                lanes = jnp.broadcast_to(lanes_at[block, group : group + 1, :], (8, LANES))
                found = [jnp.zeros((8, LANES), jnp.float32)] * 2
                for at in range(HALF):
                    one = spots[half, group, at]
                    two = spots[half, group, at + HALF]
                    values = jnp.where(
                        first, table[pl.ds(one + PAD, 8), :], table[pl.ds(two + PAD - seg_count, 8), :]
                    )
                    values = jnp.take_along_axis(values, lanes, axis=1)
                    found[at % 2] = jnp.where(place_in == at, values, found[at % 2])
                both = found[0] + found[1]
                picked = jnp.where(
                    lane[:seg_count] < HALF, both[:seg_count], both[seg_count : 2 * seg_count]
                )
                shares[block, group * seg_count : (group + 1) * seg_count, :] = (
                    picked * signs_at[block, group : group + 1, :]
                )

            @pl.when(turn_at + 2 < blocks)
            def _():
                fetch(block_at(turn_at + 2), half).start()

            if scatter:

                @pl.when(turn_at + 1 < count)
                def _():
                    share_copy(block, me).start()
        return 0

    lax.fori_loop(0, blocks // 2, pick, 0)

    def finish(chunk, _):
        each(from_own_side(chunk, place, True, True, True), sent)
        for step in range(1, lines):
            along(chunk, step, lambda todo: each(todo, sent), False)
        for at in range(lines):
            each(from_other_side(chunk, at), sent)
        return 0

    lax.fori_loop(max(0, n_chunks - 2), n_chunks, finish, 0)
    for part in range(pieces):
        for off in range(1, n_narrow):
            acts_copy(off, part).wait_send()


    if scatter:

        def take(off, total):
            return total + held[lax.rem(me + off, count)]

        others = pl.ds(0, count - 1)
        all_shares = pltpu.make_async_remote_copy(
            src_ref=shares.at[others],
            dst_ref=held.at[others],
            send_sem=share_send,
            recv_sem=share_recv,
            device_id=address(me),
            device_id_type=MESH,
        )
        all_shares.wait_recv()
        total = lax.fori_loop(1, count, take, shares[me])
        for group in range(per_block):
            out_ref[:, group * LANES : (group + 1) * LANES] = total[
                group * seg_count : (group + 1) * seg_count
            ]

        all_shares.wait_send()
    else:
        out_ref[...] = shares[...]


def body(n_wide, n_narrow, activations, cotangent, sign_bits, seg_lengths, kept_index):
    tokens = activations.shape[0] * n_narrow
    rows, cols = sign_bits.shape
    seg_count = seg_lengths.shape[0]
    kept = kept_index.shape[0]
    count = n_wide * n_narrow
    each = kept // count
    scatter = each % LANES == 0
    per_block = each // LANES if scatter else 4
    blocks = kept // LANES // per_block
    cross = 2
    row_block, col_block = min(rows, 256), min(cols, 256)
    n_chunks = cols // col_block
    windows = []
    for seg in range(seg_count):
        low = max(0, tokens - (seg_count - seg) * MOST) // TILE * TILE
        high = min(tokens, -(-(seg + 1) * MOST // TILE) * TILE)
        windows.append((low, high))
    pieces = max(1, activations.shape[0] // 512)
    anywhere = pl.BlockSpec(memory_space=pl.ANY)
    scalars = pl.BlockSpec(memory_space=pltpu.SMEM)
    vectors = pl.BlockSpec(memory_space=pltpu.VMEM)
    table = rows * cols // LANES * seg_count + 2 * PAD
    block_shape = (blocks, per_block, LANES)
    share_shape = (blocks, per_block * seg_count, LANES)
    out = (seg_count, each) if scatter else share_shape
    shares = pl.pallas_call(
        functools.partial(
            sketch_kernel, n_wide, n_narrow, cross, tuple(windows), n_chunks, scatter,
            (rows * n_wide, cols * n_narrow),
        ),
        out_shape=jax.ShapeDtypeStruct(out, jnp.float32),
        in_specs=[scalars, vectors] + [anywhere] * 3,
        out_specs=vectors,
        scratch_shapes=[
            pltpu.VMEM((tokens, rows), activations.dtype),
            pltpu.VMEM((rows, cols), sign_bits.dtype),
            pltpu.VMEM((rows, sum(high - low for low, high in windows)), jnp.bfloat16),
            pltpu.VMEM((table, LANES), jnp.float32),
            pltpu.VMEM((n_chunks, cotangent.shape[0] * n_wide, col_block), cotangent.dtype),
            pltpu.VMEM((seg_count, rows, col_block), jnp.float32),
            pltpu.VMEM((row_block, row_block), jnp.bfloat16),
            pltpu.VMEM((col_block, col_block), jnp.bfloat16),
            pltpu.VMEM(block_shape, jnp.int32),
            pltpu.VMEM(block_shape, jnp.int32),
            pltpu.VMEM(block_shape, jnp.float32),
            pltpu.SMEM((2, per_block, LANES), jnp.int32),
            pltpu.VMEM(share_shape, jnp.float32),
            pltpu.VMEM(share_shape, jnp.float32),
            pltpu.SemaphoreType.DMA((3,)),
            pltpu.SemaphoreType.DMA((2,)),
            pltpu.SemaphoreType.DMA((max(1, n_narrow - 1), pieces)),
            pltpu.SemaphoreType.DMA((max(1, n_narrow - 1), pieces)),
            pltpu.SemaphoreType.DMA((5, 2, n_wide // (2 * cross))),
            pltpu.SemaphoreType.DMA((2,)),
            pltpu.SemaphoreType.DMA((n_chunks, n_wide // 2)),
            pltpu.SemaphoreType.DMA((n_chunks,)),
            pltpu.SemaphoreType.DMA,
            pltpu.SemaphoreType.DMA,
        ],
        compiler_params=pltpu.CompilerParams(
            collective_id=0, has_side_effects=True, vmem_limit_bytes=62 * 1024 * 1024
        ),
        name="sketch",
    )(seg_lengths, kept_index.reshape(block_shape), activations, cotangent, sign_bits)
    if scatter:
        return shares
    flat = shares.reshape(blocks, per_block, seg_count, LANES)
    flat = flat.transpose(2, 0, 1, 3).reshape(seg_count, kept)
    return lax.psum_scatter(flat, ("wide", "narrow"), scatter_dimension=1, tiled=True)


def solution(mesh):
    return jax.shard_map(
        functools.partial(body, mesh.shape["wide"], mesh.shape["narrow"]),
        mesh=mesh,
        in_specs=(P("narrow", "wide"), P("wide", "narrow"), P("wide", "narrow"), P(), P()),
        out_specs=P(None, ("wide", "narrow")),
        check_vma=False,
    )
```

```python
import functools
import math

import jax
import jax.numpy as jnp
from jax import lax
from jax.experimental import pallas as pl
from jax.experimental.pallas import tpu as pltpu
from jax.sharding import PartitionSpec as P

LANES = 128
HALF = LANES // 2
MOST = 1536
TILE = 256
PAD = 8
MESH = pl.DeviceIdType.MESH


def parity(values):
    for shift in (16, 8, 4, 2, 1):
        values = values ^ lax.shift_right_logical(values, shift)
    return values & 1


def sylvester(extent):
    rows = lax.broadcasted_iota(jnp.int32, (extent, extent), 0)
    cols = lax.broadcasted_iota(jnp.int32, (extent, extent), 1)
    return (1 - 2 * parity(rows & cols)).astype(jnp.float32).astype(jnp.bfloat16)


def butterflies(parts):
    parts = list(parts)
    gap = 1
    while gap < len(parts):
        for low in range(len(parts)):
            if not low & gap:
                one, two = parts[low], parts[low | gap]
                parts[low], parts[low | gap] = one + two, one - two
        gap *= 2
    return parts


def halves(values):
    high = values.astype(jnp.bfloat16)
    low = (values - high.astype(jnp.float32)).astype(jnp.bfloat16)
    return high, low


def log2(extent):
    return extent.bit_length() - 1


def sketch_kernel(
    n_wide, n_narrow, cross, windows, n_chunks, scatter, full_shape,
    lengths, kept, acts, cots, bits_in,
    out_ref, acts_all, bits_ref, flipped, table, bufs, grads, left_ref, right_ref,
    rows_at, lanes_at, signs_at, spots, shares, held,
    local_sem, spots_sem, acts_send, acts_recv, cots_send, mate_send, cots_recv, both_recv,
    share_send, share_recv,
):
    wide = lax.axis_index("wide")
    narrow = lax.axis_index("narrow")
    count = n_wide * n_narrow
    me = wide * n_narrow + narrow
    lines = n_wide // (2 * cross)
    core = lax.rem(wide, 2)
    side = lax.rem(wide // 2, cross)
    place = wide // (2 * cross)
    mate = place + 1 - 2 * lax.rem(place, 2)
    tok_acts = acts.shape[0]
    tok_cots = cots.shape[0]
    tokens = acts_all.shape[0]
    rows, cols = bits_in.shape
    row_block = left_ref.shape[0]
    col_block = right_ref.shape[0]
    row_groups = rows // row_block
    per_group = col_block // LANES
    seg_count = len(windows)
    stretch = per_group * rows * seg_count
    blocks, per_block = kept.shape[:2]
    pieces = acts_send.shape[1]
    piece = tok_acts // pieces

    def index_of(at, across, on_core):
        return (at * cross + across) * 2 + on_core

    partner = index_of(place, side, 1 - core)
    up = index_of(lax.rem(place + 1, lines), side, core)
    down = index_of(lax.rem(place + lines - 1, lines), side, core)
    other_side = 1 - side
    over = index_of(place, other_side, core)
    mate_index = index_of(mate, side, core)
    has_up = place < lines - 1
    has_down = place > 0

    my_cots = pl.ds(wide * tok_cots, tok_cots)

    def columns_of(chunk):
        return pl.ds(pl.multiple_of(chunk * col_block, col_block), col_block)

    def own_cots(chunk):
        return pltpu.make_async_copy(
            cots.at[:, columns_of(chunk)], bufs.at[chunk, my_cots, :], local_sem.at[2]
        )

    own_acts = pltpu.make_async_copy(
        acts, acts_all.at[pl.ds(narrow * tok_acts, tok_acts), :], local_sem.at[0]
    )
    own_bits = pltpu.make_async_copy(bits_in, bits_ref, local_sem.at[1])
    for chunk in range(n_chunks):
        own_cots(chunk).start()
    own_acts.start()
    own_bits.start()

    barrier = pltpu.get_barrier_semaphore()

    def address(who):
        return {"wide": who // n_narrow, "narrow": lax.rem(who, n_narrow)}

    def greet(off, _):
        who = lax.rem(me + off, count)
        pl.semaphore_signal(barrier, inc=1, device_id=address(who), device_id_type=MESH)
        return 0

    lax.fori_loop(1, count, greet, 0)
    pl.semaphore_wait(barrier, count - 1)

    def acts_copy(off, part):
        spot = pl.multiple_of(part * piece, piece)
        return pltpu.make_async_remote_copy(
            src_ref=acts.at[pl.ds(spot, piece), :],
            dst_ref=acts_all.at[pl.ds(narrow * tok_acts + spot, piece), :],
            send_sem=acts_send.at[off - 1, part],
            recv_sem=acts_recv.at[off - 1, part],
            device_id={"narrow": lax.rem(narrow + off, n_narrow)},
            device_id_type=MESH,
        )

    def cots_copy(chunk, shard, to, send_sem, own=False):
        place_of = bufs.at[chunk, pl.ds(shard * tok_cots, tok_cots), :]
        return pltpu.make_async_remote_copy(
            src_ref=cots.at[:, columns_of(chunk)] if own else place_of,
            dst_ref=place_of,
            send_sem=send_sem,
            recv_sem=both_recv.at[chunk] if to is partner else cots_recv.at[chunk, shard // 2],
            device_id={"wide": to},
            device_id_type=MESH,
        )

    def turn(chunk):
        return core == lax.rem(chunk, 2)

    def from_own_side(chunk, at, climbs, drops, own=False):
        shard = index_of(at, side, core)
        step = lax.rem(chunk, 2)

        def to_device(way, to):
            return cots_copy(chunk, shard, to, cots_send.at[way, step, at], own)

        todo = [(lambda chunk: ~((at == mate) & turn(chunk)), to_device(3, over))]
        if climbs:
            todo.append((lambda chunk: has_up, to_device(0, up)))
        if drops:
            todo.append((lambda chunk: has_down, to_device(1, down)))
        todo.append((None, to_device(2, partner)))
        return todo

    def from_other_side(chunk, at):
        shard = index_of(at, other_side, core)
        step = lax.rem(chunk, 2)
        return [
            (
                lambda chunk: (at == place) & turn(chunk),
                cots_copy(chunk, shard, mate_index, mate_send.at[step]),
            ),
            (None, cots_copy(chunk, shard, partner, cots_send.at[4, step, at])),
        ]

    def sent(chunk, todo):
        for condition, copy in todo:
            if condition is None:
                copy.wait_send()
            else:
                pl.when(condition(chunk))(copy.wait_send)

    def start(chunk, todo):
        for condition, copy in todo:
            if condition is None:
                pl.when(chunk >= 2)(copy.wait_send)
                copy.start()
            else:
                pl.when((chunk >= 2) & condition(chunk - 2))(copy.wait_send)
                pl.when(condition(chunk))(copy.start)

    def arrived(chunk, shard):
        cots_copy(chunk, shard, up, mate_send.at[0]).wait_recv()

    def along(chunk, step, act, wait):
        @pl.when(place - step >= 0)
        def _():
            if wait:
                arrived(chunk, index_of(place - step, side, core))
            act(from_own_side(chunk, place - step, True, False))

        @pl.when(place + step < lines)
        def _():
            if wait:
                arrived(chunk, index_of(place + step, side, core))
            act(from_own_side(chunk, place + step, False, True))

    def across(chunk, step):
        for way in (1,) if step == 0 else (-1, 1):
            at = place + way * step

            @pl.when((at >= 0) & (at < lines))
            def _():
                arrived(chunk, index_of(at, other_side, core))
                start(chunk, from_other_side(chunk, at))

    def launch(chunk):
        start(chunk, from_own_side(chunk, place, True, True, True))

    starts = []
    total = 0
    for seg in range(seg_count):
        starts.append(total)
        total = total + lengths[seg]
    starts.append(total)

    def flip(begin):
        begin = pl.multiple_of(begin, TILE)
        values = acts_all[pl.ds(begin, TILE), :].astype(jnp.float32).T
        where_at = begin + lax.broadcasted_iota(jnp.int32, values.shape, 1)
        offset = 0
        for seg, (low, high) in enumerate(windows):

            @pl.when((begin >= low) & (begin < high))
            def _():
                inside = (where_at >= starts[seg]) & (where_at < starts[seg + 1])
                spot = pl.multiple_of(offset + begin - low, TILE)
                flipped[:, pl.ds(spot, TILE)] = jnp.where(inside, values, 0.0).astype(jnp.bfloat16)

            offset += high - low

    def flip_own(part, _):
        spot = narrow * tok_acts + part * piece

        def one(at, _):
            flip(spot + at * TILE)
            return 0

        return lax.fori_loop(0, piece // TILE, one, 0)

    def flip_far(part, _):
        for off in range(1, n_narrow):
            acts_copy(off, part).wait_recv()
            spot = lax.rem(narrow + n_narrow - off, n_narrow) * tok_acts + part * piece

            def one(at, _):
                flip(spot + at * TILE)
                return 0

            lax.fori_loop(0, piece // TILE, one, 0)
        return 0

    def prologue():
        left_ref[...] = sylvester(row_block)
        right_ref[...] = sylvester(col_block)
        table[pl.ds(0, PAD), :] = jnp.zeros((PAD, LANES), jnp.float32)
        table[pl.ds(PAD + n_chunks * stretch, PAD), :] = jnp.zeros((PAD, LANES), jnp.float32)
        full_rows, full_cols = full_shape
        scale = 1.0 / math.sqrt(full_rows * full_cols)
        index = kept[...]
        row_of = lax.shift_right_logical(index, log2(full_cols))
        col_of = index & (full_cols - 1)
        common = lax.shift_right_logical(row_of, log2(rows)) & wide
        odd = parity(common) ^ parity(lax.shift_right_logical(col_of, log2(cols)) & narrow)
        signs_at[...] = (1 - 2 * odd).astype(jnp.float32) * scale
        col = col_of & (cols - 1)
        lane_block = lax.shift_right_logical(col, log2(LANES))
        rows_at[...] = (lane_block * rows + (row_of & (rows - 1))) * seg_count
        lanes_at[...] = col & (LANES - 1)

    def multiply(chunk):
        half_rows = bufs.at[chunk, pl.ds(0, tokens // 2), :]
        pltpu.make_async_remote_copy(
            src_ref=half_rows,
            dst_ref=half_rows,
            send_sem=mate_send.at[0],
            recv_sem=both_recv.at[chunk],
            device_id={"wide": partner},
            device_id_type=MESH,
        ).wait_recv()

        columns = columns_of(chunk)
        offset = 0
        for seg, (low, high) in enumerate(windows):
            grads[seg] = jnp.dot(
                flipped[:, offset : offset + high - low],
                bufs[chunk, low:high, :],
                preferred_element_type=jnp.float32,
            )
            offset += high - low

    def transform(chunk):
        columns = columns_of(chunk)
        for seg in range(seg_count):
            gain = lax.rsqrt(jnp.full((1, col_block), lengths[seg], jnp.int32).astype(jnp.float32))
            sign = (1 - 2 * bits_ref[:, columns]).astype(jnp.float32)
            grad = grads[seg] * (sign * gain)
            parts = [
                grad[group * row_block : (group + 1) * row_block]
                for group in range(row_groups)
            ]
            for group, part in enumerate(butterflies(parts)):
                upper, lower = halves(part)
                mixed = jnp.dot(
                    left_ref[...], upper, preferred_element_type=jnp.float32
                ) + jnp.dot(left_ref[...], lower, preferred_element_type=jnp.float32)
                upper, lower = halves(mixed)
                mixed = jnp.dot(
                    upper, right_ref[...], preferred_element_type=jnp.float32
                ) + jnp.dot(lower, right_ref[...], preferred_element_type=jnp.float32)
                for lane_block in range(per_group):
                    block = chunk * per_group + lane_block
                    base = PAD + (block * rows + group * row_block) * seg_count + seg
                    table[pl.ds(base, row_block, stride=seg_count), :] = mixed[
                        :, lane_block * LANES : (lane_block + 1) * LANES
                    ]

    for part in range(pieces):
        for off in range(1, n_narrow):
            acts_copy(off, part).start()

    def inside(chunk):
        return (chunk >= 0) & (chunk < n_chunks)

    def relay(chunk, step):
        @pl.when(inside(chunk))
        def _():
            along(chunk, step, functools.partial(start, chunk), True)

    def accept(chunk, step):
        @pl.when(inside(chunk))
        def _():
            across(chunk, step)

    begun = 3 * (pieces + 3) + 1

    def ready(at, units):
        slot = at // 3 - 2
        reach = jnp.where(at % 3 == 2, slot - lines + 1, slot - lines)
        return (at >= begun) & (units < 2 * n_chunks) & (units // 2 <= reach)

    def work(at, units):
        slot = at // 3 - 2
        phase = at % 3

        @pl.when(phase == 0)
        def _():
            for step in range(min(2, lines - 1), 0, -1):
                accept(slot - 3, step)
                if step == 2:
                    relay(slot - 1, 1)
            for step in range(lines - 1, 2, -1):
                accept(slot - step, step)

        @pl.when(phase == 1)
        def _():
            accept(slot - 2, 0)

            @pl.when(inside(slot + 2))
            def _():
                launch(slot + 2)

            @pl.when(slot == -2)
            def _():
                prologue()
                own_acts.wait()

            near = slot + 2
            lax.fori_loop(
                lax.clamp(0, near, pieces), lax.clamp(0, near + 1, pieces), flip_own, 0
            )
            far = slot - 2
            lax.fori_loop(lax.clamp(0, far, pieces), lax.clamp(0, far + 1, pieces), flip_far, 0)

            for step in range(lines - 1, 2, -1):
                relay(slot + 1 - step, step)

        @pl.when(phase == 2)
        def _():
            relay(slot - 1, 2)

        @pl.when(at == begun)
        def _():
            own_bits.wait()
            pltpu.make_async_copy(
                bufs.at[:, my_cots, :], bufs.at[:, my_cots, :], local_sem.at[2]
            ).wait()

        go = ready(at, units)
        pl.when(go & (units % 2 == 0))(lambda: multiply(units // 2))
        pl.when(go & (units % 2 == 1))(lambda: transform(units // 2))
        return units + jnp.where(go, 1, 0)

    last, units = 0, 0
    while units < 2 * n_chunks or last < 3 * (n_chunks + lines + 1) + 1:
        slot = last // 3 - 2
        reach = slot - lines + 1 if last % 3 == 2 else slot - lines
        if last >= begun and units < 2 * n_chunks and units // 2 <= reach:
            units += 1
        last += 1
    lax.fori_loop(0, last, work, 0)

    def fetch(block, half):
        return pltpu.make_async_copy(rows_at.at[block], spots.at[half], spots_sem.at[half])

    def block_at(turn_at):
        return lax.rem(me + turn_at + 1, count) if scatter else turn_at

    for half in range(2):
        fetch(block_at(half), half).start()

    def join(at, _):
        base = pl.multiple_of(PAD + at * 8, 8)
        spans = [pl.ds(base + chunk * stretch, 8) for chunk in range(n_chunks)]
        parts = butterflies([table[span, :] for span in spans])
        for span, part in zip(spans, parts):
            table[span, :] = part
        return 0

    lax.fori_loop(0, stretch // 8, join, 0, unroll=4)

    lane = lax.broadcasted_iota(jnp.int32, (8, LANES), 1)
    row = lax.broadcasted_iota(jnp.int32, (8, LANES), 0)
    first = row < seg_count
    place_in = lane & (HALF - 1)

    def share_copy(who, slot):
        return pltpu.make_async_remote_copy(
            src_ref=shares.at[who],
            dst_ref=held.at[slot],
            send_sem=share_send,
            recv_sem=share_recv,
            device_id=address(who),
            device_id_type=MESH,
        )

    def pick(pair, _):
        for half in range(2):
            turn_at = pair * 2 + half
            block = block_at(turn_at)
            fetch(block, half).wait()
            for group in range(per_block):
                lanes = jnp.broadcast_to(lanes_at[block, group : group + 1, :], (8, LANES))
                found = [jnp.zeros((8, LANES), jnp.float32)] * 2
                for at in range(HALF):
                    one = spots[half, group, at]
                    two = spots[half, group, at + HALF]
                    values = jnp.where(
                        first, table[pl.ds(one + PAD, 8), :], table[pl.ds(two + PAD - seg_count, 8), :]
                    )
                    values = jnp.take_along_axis(values, lanes, axis=1)
                    found[at % 2] = jnp.where(place_in == at, values, found[at % 2])
                both = found[0] + found[1]
                picked = jnp.where(
                    lane[:seg_count] < HALF, both[:seg_count], both[seg_count : 2 * seg_count]
                )
                shares[block, group * seg_count : (group + 1) * seg_count, :] = (
                    picked * signs_at[block, group : group + 1, :]
                )

            @pl.when(turn_at + 2 < blocks)
            def _():
                fetch(block_at(turn_at + 2), half).start()

            if scatter:

                @pl.when(turn_at + 1 < count)
                def _():
                    share_copy(block, me).start()
        return 0

    lax.fori_loop(0, blocks // 2, pick, 0)

    def finish(chunk, _):
        sent(chunk, from_own_side(chunk, place, True, True, True))
        for step in range(1, lines):
            along(chunk, step, functools.partial(sent, chunk), False)
        for at in range(lines):
            sent(chunk, from_other_side(chunk, at))
        return 0

    lax.fori_loop(max(0, n_chunks - 2), n_chunks, finish, 0)
    for part in range(pieces):
        for off in range(1, n_narrow):
            acts_copy(off, part).wait_send()


    if scatter:

        def take(off, total):
            return total + held[lax.rem(me + off, count)]

        others = pl.ds(0, count - 1)
        all_shares = pltpu.make_async_remote_copy(
            src_ref=shares.at[others],
            dst_ref=held.at[others],
            send_sem=share_send,
            recv_sem=share_recv,
            device_id=address(me),
            device_id_type=MESH,
        )
        all_shares.wait_recv()
        total = lax.fori_loop(1, count, take, shares[me])
        for group in range(per_block):
            out_ref[:, group * LANES : (group + 1) * LANES] = total[
                group * seg_count : (group + 1) * seg_count
            ]

        all_shares.wait_send()
    else:
        out_ref[...] = shares[...]


def body(n_wide, n_narrow, activations, cotangent, sign_bits, seg_lengths, kept_index):
    tokens = activations.shape[0] * n_narrow
    rows, cols = sign_bits.shape
    seg_count = seg_lengths.shape[0]
    kept = kept_index.shape[0]
    count = n_wide * n_narrow
    each = kept // count
    scatter = each % LANES == 0
    per_block = each // LANES if scatter else 4
    blocks = kept // LANES // per_block
    cross = 2
    row_block, col_block = min(rows, 256), min(cols, 256)
    n_chunks = cols // col_block
    windows = []
    for seg in range(seg_count):
        low = max(0, tokens - (seg_count - seg) * MOST) // TILE * TILE
        high = min(tokens, -(-(seg + 1) * MOST // TILE) * TILE)
        windows.append((low, high))
    pieces = max(1, activations.shape[0] // 512)
    anywhere = pl.BlockSpec(memory_space=pl.ANY)
    scalars = pl.BlockSpec(memory_space=pltpu.SMEM)
    vectors = pl.BlockSpec(memory_space=pltpu.VMEM)
    table = rows * cols // LANES * seg_count + 2 * PAD
    block_shape = (blocks, per_block, LANES)
    share_shape = (blocks, per_block * seg_count, LANES)
    out = (seg_count, each) if scatter else share_shape
    shares = pl.pallas_call(
        functools.partial(
            sketch_kernel, n_wide, n_narrow, cross, tuple(windows), n_chunks, scatter,
            (rows * n_wide, cols * n_narrow),
        ),
        out_shape=jax.ShapeDtypeStruct(out, jnp.float32),
        in_specs=[scalars, vectors] + [anywhere] * 3,
        out_specs=vectors,
        scratch_shapes=[
            pltpu.VMEM((tokens, rows), activations.dtype),
            pltpu.VMEM((rows, cols), sign_bits.dtype),
            pltpu.VMEM((rows, sum(high - low for low, high in windows)), jnp.bfloat16),
            pltpu.VMEM((table, LANES), jnp.float32),
            pltpu.VMEM((n_chunks, cotangent.shape[0] * n_wide, col_block), cotangent.dtype),
            pltpu.VMEM((seg_count, rows, col_block), jnp.float32),
            pltpu.VMEM((row_block, row_block), jnp.bfloat16),
            pltpu.VMEM((col_block, col_block), jnp.bfloat16),
            pltpu.VMEM(block_shape, jnp.int32),
            pltpu.VMEM(block_shape, jnp.int32),
            pltpu.VMEM(block_shape, jnp.float32),
            pltpu.SMEM((2, per_block, LANES), jnp.int32),
            pltpu.VMEM(share_shape, jnp.float32),
            pltpu.VMEM(share_shape, jnp.float32),
            pltpu.SemaphoreType.DMA((3,)),
            pltpu.SemaphoreType.DMA((2,)),
            pltpu.SemaphoreType.DMA((max(1, n_narrow - 1), pieces)),
            pltpu.SemaphoreType.DMA((max(1, n_narrow - 1), pieces)),
            pltpu.SemaphoreType.DMA((5, 2, n_wide // (2 * cross))),
            pltpu.SemaphoreType.DMA((2,)),
            pltpu.SemaphoreType.DMA((n_chunks, n_wide // 2)),
            pltpu.SemaphoreType.DMA((n_chunks,)),
            pltpu.SemaphoreType.DMA,
            pltpu.SemaphoreType.DMA,
        ],
        compiler_params=pltpu.CompilerParams(
            collective_id=0, has_side_effects=True, vmem_limit_bytes=62 * 1024 * 1024
        ),
        name="sketch",
    )(seg_lengths, kept_index.reshape(block_shape), activations, cotangent, sign_bits)
    if scatter:
        return shares
    flat = shares.reshape(blocks, per_block, seg_count, LANES)
    flat = flat.transpose(2, 0, 1, 3).reshape(seg_count, kept)
    return lax.psum_scatter(flat, ("wide", "narrow"), scatter_dimension=1, tiled=True)


def solution(mesh):
    return jax.shard_map(
        functools.partial(body, mesh.shape["wide"], mesh.shape["narrow"]),
        mesh=mesh,
        in_specs=(P("narrow", "wide"), P("wide", "narrow"), P("wide", "narrow"), P(), P()),
        out_specs=P(None, ("wide", "narrow")),
        check_vma=False,
    )
```

```python
import functools
import math

import jax
import jax.numpy as jnp
from jax import lax
from jax.experimental import pallas as pl
from jax.experimental.pallas import tpu as pltpu
from jax.sharding import PartitionSpec as P

LANES = 128
HALF = LANES // 2
MOST = 1536
TILE = 256
PAD = 8
RUN = 2
BUFFERS = 2 * RUN
MESH = pl.DeviceIdType.MESH


def parity(values):
    for shift in (16, 8, 4, 2, 1):
        values = values ^ lax.shift_right_logical(values, shift)
    return values & 1


def sylvester(extent):
    rows = lax.broadcasted_iota(jnp.int32, (extent, extent), 0)
    cols = lax.broadcasted_iota(jnp.int32, (extent, extent), 1)
    return (1 - 2 * parity(rows & cols)).astype(jnp.float32).astype(jnp.bfloat16)


def butterflies(parts):
    parts = list(parts)
    gap = 1
    while gap < len(parts):
        for low in range(len(parts)):
            if not low & gap:
                one, two = parts[low], parts[low | gap]
                parts[low], parts[low | gap] = one + two, one - two
        gap *= 2
    return parts


def halves(values):
    high = values.astype(jnp.bfloat16)
    low = (values - high.astype(jnp.float32)).astype(jnp.bfloat16)
    return high, low


def log2(extent):
    return extent.bit_length() - 1


def sketch_kernel(
    n_wide, n_narrow, cross, windows, n_chunks, scatter, full_shape,
    lengths, kept, acts, cots, bits_in,
    out_ref, acts_all, bits_ref, flipped, table, bufs, grads, left_ref, right_ref,
    rows_at, lanes_at, signs_at, spots, shares, held,
    local_sem, spots_sem, acts_send, acts_recv, cots_send, mate_send, cots_recv, both_recv,
    share_send, share_recv,
):
    wide = lax.axis_index("wide")
    narrow = lax.axis_index("narrow")
    count = n_wide * n_narrow
    me = wide * n_narrow + narrow
    lines = n_wide // (2 * cross)
    core = lax.rem(wide, 2)
    side = lax.rem(wide // 2, cross)
    place = wide // (2 * cross)
    mate = place + 1 - 2 * lax.rem(place, 2)
    tok_acts = acts.shape[0]
    tok_cots = cots.shape[0]
    tokens = acts_all.shape[0]
    rows, cols = bits_in.shape
    row_block = left_ref.shape[0]
    col_block = right_ref.shape[0]
    row_groups = rows // row_block
    per_group = col_block // LANES
    seg_count = len(windows)
    stretch = per_group * rows * seg_count
    blocks, per_block = kept.shape[:2]
    pieces = acts_send.shape[1]
    piece = tok_acts // pieces

    def index_of(at, across, on_core):
        return (at * cross + across) * 2 + on_core

    partner = index_of(place, side, 1 - core)
    up = index_of(lax.rem(place + 1, lines), side, core)
    down = index_of(lax.rem(place + lines - 1, lines), side, core)
    other_side = 1 - side
    over = index_of(place, other_side, core)
    mate_index = index_of(mate, side, core)
    has_up = place < lines - 1
    has_down = place > 0

    my_cots = pl.ds(wide * tok_cots, tok_cots)

    def columns_of(chunk):
        return pl.ds(pl.multiple_of(chunk * col_block, col_block), col_block)

    def own_cots(chunk):
        return pltpu.make_async_copy(
            cots.at[:, columns_of(chunk)], bufs.at[chunk, my_cots, :], local_sem.at[2]
        )

    own_acts = pltpu.make_async_copy(
        acts, acts_all.at[pl.ds(narrow * tok_acts, tok_acts), :], local_sem.at[0]
    )
    own_bits = pltpu.make_async_copy(bits_in, bits_ref, local_sem.at[1])
    for chunk in range(n_chunks):
        own_cots(chunk).start()
    own_acts.start()
    own_bits.start()

    barrier = pltpu.get_barrier_semaphore()

    def address(who):
        return {"wide": who // n_narrow, "narrow": lax.rem(who, n_narrow)}

    def greet(off, _):
        who = lax.rem(me + off, count)
        pl.semaphore_signal(barrier, inc=1, device_id=address(who), device_id_type=MESH)
        return 0

    lax.fori_loop(1, count, greet, 0)
    pl.semaphore_wait(barrier, count - 1)

    def acts_copy(off, part):
        spot = pl.multiple_of(part * piece, piece)
        return pltpu.make_async_remote_copy(
            src_ref=acts.at[pl.ds(spot, piece), :],
            dst_ref=acts_all.at[pl.ds(narrow * tok_acts + spot, piece), :],
            send_sem=acts_send.at[off - 1, part],
            recv_sem=acts_recv.at[off - 1, part],
            device_id={"narrow": lax.rem(narrow + off, n_narrow)},
            device_id_type=MESH,
        )

    def cots_copy(chunk, shard, to, send_sem, own=False):
        place_of = bufs.at[chunk, pl.ds(shard * tok_cots, tok_cots), :]
        return pltpu.make_async_remote_copy(
            src_ref=cots.at[:, columns_of(chunk)] if own else place_of,
            dst_ref=place_of,
            send_sem=send_sem,
            recv_sem=both_recv.at[chunk] if to is partner else cots_recv.at[chunk, shard // 2],
            device_id={"wide": to},
            device_id_type=MESH,
        )

    def turn(chunk):
        return core == lax.rem(chunk, 2)

    def from_own_side(chunk, at, climbs, drops, own=False):
        shard = index_of(at, side, core)
        step = lax.rem(chunk, 2)

        def to_device(way, to):
            return cots_copy(chunk, shard, to, cots_send.at[way, step, at], own)

        todo = [(lambda chunk: ~((at == mate) & turn(chunk)), to_device(3, over))]
        if climbs:
            todo.append((lambda chunk: has_up, to_device(0, up)))
        if drops:
            todo.append((lambda chunk: has_down, to_device(1, down)))
        todo.append((None, to_device(2, partner)))
        return todo

    def from_other_side(chunk, at):
        shard = index_of(at, other_side, core)
        step = lax.rem(chunk, 2)
        return [
            (
                lambda chunk: (at == place) & turn(chunk),
                cots_copy(chunk, shard, mate_index, mate_send.at[step]),
            ),
            (None, cots_copy(chunk, shard, partner, cots_send.at[4, step, at])),
        ]

    def sent(chunk, todo):
        for condition, copy in todo:
            if condition is None:
                copy.wait_send()
            else:
                pl.when(condition(chunk))(copy.wait_send)

    def start(chunk, todo):
        for condition, copy in todo:
            if condition is None:
                pl.when(chunk >= 2)(copy.wait_send)
                copy.start()
            else:
                pl.when((chunk >= 2) & condition(chunk - 2))(copy.wait_send)
                pl.when(condition(chunk))(copy.start)

    def arrived(chunk, shard):
        cots_copy(chunk, shard, up, mate_send.at[0]).wait_recv()

    def along(chunk, step, act, wait):
        @pl.when(place - step >= 0)
        def _():
            if wait:
                arrived(chunk, index_of(place - step, side, core))
            act(from_own_side(chunk, place - step, True, False))

        @pl.when(place + step < lines)
        def _():
            if wait:
                arrived(chunk, index_of(place + step, side, core))
            act(from_own_side(chunk, place + step, False, True))

    def across(chunk, step):
        for way in (1,) if step == 0 else (-1, 1):
            at = place + way * step

            @pl.when((at >= 0) & (at < lines))
            def _():
                arrived(chunk, index_of(at, other_side, core))
                start(chunk, from_other_side(chunk, at))

    def launch(chunk):
        start(chunk, from_own_side(chunk, place, True, True, True))

    starts = []
    total = 0
    for seg in range(seg_count):
        starts.append(total)
        total = total + lengths[seg]
    starts.append(total)

    def flip(begin):
        begin = pl.multiple_of(begin, TILE)
        values = acts_all[pl.ds(begin, TILE), :].astype(jnp.float32).T
        where_at = begin + lax.broadcasted_iota(jnp.int32, values.shape, 1)
        offset = 0
        for seg, (low, high) in enumerate(windows):

            @pl.when((begin >= low) & (begin < high))
            def _():
                inside = (where_at >= starts[seg]) & (where_at < starts[seg + 1])
                spot = pl.multiple_of(offset + begin - low, TILE)
                flipped[:, pl.ds(spot, TILE)] = jnp.where(inside, values, 0.0).astype(jnp.bfloat16)

            offset += high - low

    def flip_own(part, _):
        spot = narrow * tok_acts + part * piece

        def one(at, _):
            flip(spot + at * TILE)
            return 0

        return lax.fori_loop(0, piece // TILE, one, 0)

    def flip_far(part, _):
        for off in range(1, n_narrow):
            acts_copy(off, part).wait_recv()
            spot = lax.rem(narrow + n_narrow - off, n_narrow) * tok_acts + part * piece

            def one(at, _):
                flip(spot + at * TILE)
                return 0

            lax.fori_loop(0, piece // TILE, one, 0)
        return 0

    def prologue():
        left_ref[...] = sylvester(row_block)
        right_ref[...] = sylvester(col_block)
        table[pl.ds(0, PAD), :] = jnp.zeros((PAD, LANES), jnp.float32)
        table[pl.ds(PAD + n_chunks * stretch, PAD), :] = jnp.zeros((PAD, LANES), jnp.float32)
        full_rows, full_cols = full_shape
        scale = 1.0 / math.sqrt(full_rows * full_cols)
        index = kept[...]
        row_of = lax.shift_right_logical(index, log2(full_cols))
        col_of = index & (full_cols - 1)
        common = lax.shift_right_logical(row_of, log2(rows)) & wide
        odd = parity(common) ^ parity(lax.shift_right_logical(col_of, log2(cols)) & narrow)
        signs_at[...] = (1 - 2 * odd).astype(jnp.float32) * scale
        col = col_of & (cols - 1)
        lane_block = lax.shift_right_logical(col, log2(LANES))
        rows_at[...] = (lane_block * rows + (row_of & (rows - 1))) * seg_count
        lanes_at[...] = col & (LANES - 1)

    def multiply(chunk):
        half_rows = bufs.at[chunk, pl.ds(0, tokens // 2), :]
        pltpu.make_async_remote_copy(
            src_ref=half_rows,
            dst_ref=half_rows,
            send_sem=mate_send.at[0],
            recv_sem=both_recv.at[chunk],
            device_id={"wide": partner},
            device_id_type=MESH,
        ).wait_recv()

        columns = columns_of(chunk)
        offset = 0
        for seg, (low, high) in enumerate(windows):
            grads[seg] = jnp.dot(
                flipped[:, offset : offset + high - low],
                bufs[chunk, low:high, :],
                preferred_element_type=jnp.float32,
            )
            offset += high - low

    def transform(chunk):
        columns = columns_of(chunk)
        for seg in range(seg_count):
            gain = lax.rsqrt(jnp.full((1, col_block), lengths[seg], jnp.int32).astype(jnp.float32))
            sign = (1 - 2 * bits_ref[:, columns]).astype(jnp.float32)
            grad = grads[seg] * (sign * gain)
            parts = [
                grad[group * row_block : (group + 1) * row_block]
                for group in range(row_groups)
            ]
            for group, part in enumerate(butterflies(parts)):
                upper, lower = halves(part)
                mixed = jnp.dot(
                    left_ref[...], upper, preferred_element_type=jnp.float32
                ) + jnp.dot(left_ref[...], lower, preferred_element_type=jnp.float32)
                upper, lower = halves(mixed)
                mixed = jnp.dot(
                    upper, right_ref[...], preferred_element_type=jnp.float32
                ) + jnp.dot(lower, right_ref[...], preferred_element_type=jnp.float32)
                for lane_block in range(per_group):
                    block = chunk * per_group + lane_block
                    base = PAD + (block * rows + group * row_block) * seg_count + seg
                    table[pl.ds(base, row_block, stride=seg_count), :] = mixed[
                        :, lane_block * LANES : (lane_block + 1) * LANES
                    ]

    for part in range(pieces):
        for off in range(1, n_narrow):
            acts_copy(off, part).start()

    def inside(chunk):
        return (chunk >= 0) & (chunk < n_chunks)

    def relay(chunk, step):
        @pl.when(inside(chunk))
        def _():
            along(chunk, step, functools.partial(start, chunk), True)

    def accept(chunk, step):
        @pl.when(inside(chunk))
        def _():
            across(chunk, step)

    begun = 3 * (pieces + 3) + 1

    def ready(at, units):
        slot = at // 3 - 2
        reach = jnp.where(at % 3 == 2, slot - lines + 1, slot - lines)
        return (at >= begun) & (units < 2 * n_chunks) & (units // 2 <= reach)

    def work(at, units):
        slot = at // 3 - 2
        phase = at % 3

        @pl.when(phase == 0)
        def _():
            for step in range(min(2, lines - 1), 0, -1):
                accept(slot - 3, step)
                if step == 2:
                    relay(slot - 1, 1)
            for step in range(lines - 1, 2, -1):
                accept(slot - step, step)

        @pl.when(phase == 1)
        def _():
            accept(slot - 2, 0)

            @pl.when(inside(slot + 2))
            def _():
                launch(slot + 2)

            @pl.when(slot == -2)
            def _():
                prologue()
                own_acts.wait()

            near = slot + 2
            lax.fori_loop(
                lax.clamp(0, near, pieces), lax.clamp(0, near + 1, pieces), flip_own, 0
            )
            far = slot - 2
            lax.fori_loop(lax.clamp(0, far, pieces), lax.clamp(0, far + 1, pieces), flip_far, 0)

            for step in range(lines - 1, 2, -1):
                relay(slot + 1 - step, step)

        @pl.when(phase == 2)
        def _():
            relay(slot - 1, 2)

        @pl.when(at == begun)
        def _():
            own_bits.wait()
            pltpu.make_async_copy(
                bufs.at[:, my_cots, :], bufs.at[:, my_cots, :], local_sem.at[2]
            ).wait()

        go = ready(at, units)
        pl.when(go & (units % 2 == 0))(lambda: multiply(units // 2))
        pl.when(go & (units % 2 == 1))(lambda: transform(units // 2))
        return units + jnp.where(go, 1, 0)

    last, units = 0, 0
    while units < 2 * n_chunks or last < 3 * (n_chunks + lines + 1) + 1:
        slot = last // 3 - 2
        reach = slot - lines + 1 if last % 3 == 2 else slot - lines
        if last >= begun and units < 2 * n_chunks and units // 2 <= reach:
            units += 1
        last += 1
    lax.fori_loop(0, last, work, 0)

    def fetch(block, half):
        return pltpu.make_async_copy(rows_at.at[block], spots.at[half], spots_sem.at[half])

    def block_at(turn_at):
        return lax.rem(me + turn_at + 1, count) if scatter else turn_at

    for half in range(BUFFERS):
        fetch(block_at(half), half).start()

    def join(at, _):
        base = pl.multiple_of(PAD + at * 8, 8)
        spans = [pl.ds(base + chunk * stretch, 8) for chunk in range(n_chunks)]
        parts = butterflies([table[span, :] for span in spans])
        for span, part in zip(spans, parts):
            table[span, :] = part
        return 0

    lax.fori_loop(0, stretch // 8, join, 0, unroll=4)

    lane = lax.broadcasted_iota(jnp.int32, (8, LANES), 1)
    row = lax.broadcasted_iota(jnp.int32, (8, LANES), 0)
    first = row < seg_count
    place_in = lane & (HALF - 1)

    def share_copy(who, slot):
        return pltpu.make_async_remote_copy(
            src_ref=shares.at[who],
            dst_ref=held.at[slot],
            send_sem=share_send,
            recv_sem=share_recv,
            device_id=address(who),
            device_id_type=MESH,
        )

    def pick_block(block, half):
        for group in range(per_block):
            lanes = jnp.broadcast_to(lanes_at[block, group : group + 1, :], (8, LANES))
            found = [jnp.zeros((8, LANES), jnp.float32)] * 2
            for at in range(HALF):
                one = spots[half, group, at]
                two = spots[half, group, at + HALF]
                values = jnp.where(
                    first, table[pl.ds(one + PAD, 8), :], table[pl.ds(two + PAD - seg_count, 8), :]
                )
                values = jnp.take_along_axis(values, lanes, axis=1)
                found[at % 2] = jnp.where(place_in == at, values, found[at % 2])
            both = found[0] + found[1]
            picked = jnp.where(
                lane[:seg_count] < HALF, both[:seg_count], both[seg_count : 2 * seg_count]
            )
            shares[block, group * seg_count : (group + 1) * seg_count, :] = (
                picked * signs_at[block, group : group + 1, :]
            )

    def pick(pair, _):
        for run in range(2):
            halves_at = range(run * RUN, (run + 1) * RUN)
            for half in halves_at:
                fetch(block_at(pair * BUFFERS + half), half).wait()
            for half in halves_at:
                pick_block(block_at(pair * BUFFERS + half), half)

            @pl.when(pair + 1 < blocks // BUFFERS)
            def _():
                for half in halves_at:
                    fetch(block_at((pair + 1) * BUFFERS + half), half).start()

            if scatter:
                for half in halves_at:
                    turn_at = pair * BUFFERS + half

                    @pl.when(turn_at + 1 < count)
                    def _():
                        share_copy(block_at(turn_at), me).start()
        return 0

    lax.fori_loop(0, blocks // BUFFERS, pick, 0)

    def finish(chunk, _):
        sent(chunk, from_own_side(chunk, place, True, True, True))
        for step in range(1, lines):
            along(chunk, step, functools.partial(sent, chunk), False)
        for at in range(lines):
            sent(chunk, from_other_side(chunk, at))
        return 0

    lax.fori_loop(max(0, n_chunks - 2), n_chunks, finish, 0)
    for part in range(pieces):
        for off in range(1, n_narrow):
            acts_copy(off, part).wait_send()


    if scatter:

        def take(off, total):
            return total + held[lax.rem(me + off, count)]

        others = pl.ds(0, count - 1)
        all_shares = pltpu.make_async_remote_copy(
            src_ref=shares.at[others],
            dst_ref=held.at[others],
            send_sem=share_send,
            recv_sem=share_recv,
            device_id=address(me),
            device_id_type=MESH,
        )
        all_shares.wait_recv()
        total = lax.fori_loop(1, count, take, shares[me])
        for group in range(per_block):
            out_ref[:, group * LANES : (group + 1) * LANES] = total[
                group * seg_count : (group + 1) * seg_count
            ]

        all_shares.wait_send()
    else:
        out_ref[...] = shares[...]


def body(n_wide, n_narrow, activations, cotangent, sign_bits, seg_lengths, kept_index):
    tokens = activations.shape[0] * n_narrow
    rows, cols = sign_bits.shape
    seg_count = seg_lengths.shape[0]
    kept = kept_index.shape[0]
    count = n_wide * n_narrow
    each = kept // count
    scatter = each % LANES == 0
    per_block = each // LANES if scatter else 4
    blocks = kept // LANES // per_block
    cross = 2
    row_block, col_block = min(rows, 256), min(cols, 256)
    n_chunks = cols // col_block
    windows = []
    for seg in range(seg_count):
        low = max(0, tokens - (seg_count - seg) * MOST) // TILE * TILE
        high = min(tokens, -(-(seg + 1) * MOST // TILE) * TILE)
        windows.append((low, high))
    pieces = max(1, activations.shape[0] // 512)
    anywhere = pl.BlockSpec(memory_space=pl.ANY)
    scalars = pl.BlockSpec(memory_space=pltpu.SMEM)
    vectors = pl.BlockSpec(memory_space=pltpu.VMEM)
    table = rows * cols // LANES * seg_count + 2 * PAD
    block_shape = (blocks, per_block, LANES)
    share_shape = (blocks, per_block * seg_count, LANES)
    out = (seg_count, each) if scatter else share_shape
    shares = pl.pallas_call(
        functools.partial(
            sketch_kernel, n_wide, n_narrow, cross, tuple(windows), n_chunks, scatter,
            (rows * n_wide, cols * n_narrow),
        ),
        out_shape=jax.ShapeDtypeStruct(out, jnp.float32),
        in_specs=[scalars, vectors] + [anywhere] * 3,
        out_specs=vectors,
        scratch_shapes=[
            pltpu.VMEM((tokens, rows), activations.dtype),
            pltpu.VMEM((rows, cols), sign_bits.dtype),
            pltpu.VMEM((rows, sum(high - low for low, high in windows)), jnp.bfloat16),
            pltpu.VMEM((table, LANES), jnp.float32),
            pltpu.VMEM((n_chunks, cotangent.shape[0] * n_wide, col_block), cotangent.dtype),
            pltpu.VMEM((seg_count, rows, col_block), jnp.float32),
            pltpu.VMEM((row_block, row_block), jnp.bfloat16),
            pltpu.VMEM((col_block, col_block), jnp.bfloat16),
            pltpu.VMEM(block_shape, jnp.int32),
            pltpu.VMEM(block_shape, jnp.int32),
            pltpu.VMEM(block_shape, jnp.float32),
            pltpu.SMEM((BUFFERS, per_block, LANES), jnp.int32),
            pltpu.VMEM(share_shape, jnp.float32),
            pltpu.VMEM(share_shape, jnp.float32),
            pltpu.SemaphoreType.DMA((3,)),
            pltpu.SemaphoreType.DMA((BUFFERS,)),
            pltpu.SemaphoreType.DMA((max(1, n_narrow - 1), pieces)),
            pltpu.SemaphoreType.DMA((max(1, n_narrow - 1), pieces)),
            pltpu.SemaphoreType.DMA((5, 2, n_wide // (2 * cross))),
            pltpu.SemaphoreType.DMA((2,)),
            pltpu.SemaphoreType.DMA((n_chunks, n_wide // 2)),
            pltpu.SemaphoreType.DMA((n_chunks,)),
            pltpu.SemaphoreType.DMA,
            pltpu.SemaphoreType.DMA,
        ],
        compiler_params=pltpu.CompilerParams(
            collective_id=0, has_side_effects=True, vmem_limit_bytes=62 * 1024 * 1024
        ),
        name="sketch",
    )(seg_lengths, kept_index.reshape(block_shape), activations, cotangent, sign_bits)
    if scatter:
        return shares
    flat = shares.reshape(blocks, per_block, seg_count, LANES)
    flat = flat.transpose(2, 0, 1, 3).reshape(seg_count, kept)
    return lax.psum_scatter(flat, ("wide", "narrow"), scatter_dimension=1, tiled=True)


def solution(mesh):
    return jax.shard_map(
        functools.partial(body, mesh.shape["wide"], mesh.shape["narrow"]),
        mesh=mesh,
        in_specs=(P("narrow", "wide"), P("wide", "narrow"), P("wide", "narrow"), P(), P()),
        out_specs=P(None, ("wide", "narrow")),
        check_vma=False,
    )
```

```python
import functools
import math

import jax
import jax.numpy as jnp
from jax import lax
from jax.experimental import pallas as pl
from jax.experimental.pallas import tpu as pltpu
from jax.sharding import PartitionSpec as P

LANES = 128
HALF = LANES // 2
MOST = 1536
TILE = 256
PAD = 8
RUN = 2
BUFFERS = 2 * RUN
MESH = pl.DeviceIdType.MESH


def parity(values):
    for shift in (16, 8, 4, 2, 1):
        values = values ^ lax.shift_right_logical(values, shift)
    return values & 1


def sylvester(extent):
    rows = lax.broadcasted_iota(jnp.int32, (extent, extent), 0)
    cols = lax.broadcasted_iota(jnp.int32, (extent, extent), 1)
    return (1 - 2 * parity(rows & cols)).astype(jnp.float32).astype(jnp.bfloat16)


def butterflies(parts):
    parts = list(parts)
    gap = 1
    while gap < len(parts):
        for low in range(len(parts)):
            if not low & gap:
                one, two = parts[low], parts[low | gap]
                parts[low], parts[low | gap] = one + two, one - two
        gap *= 2
    return parts


def halves(values):
    high = values.astype(jnp.bfloat16)
    low = (values - high.astype(jnp.float32)).astype(jnp.bfloat16)
    return high, low


def log2(extent):
    return extent.bit_length() - 1


def sketch_kernel(
    n_wide, n_narrow, cross, windows, n_chunks, scatter, full_shape,
    lengths, kept, acts, cots, bits_in,
    out_ref, acts_all, bits_ref, flipped, table, bufs, grads, left_ref, right_ref,
    rows_at, lanes_at, signs_at, spots, shares, held,
    local_sem, spots_sem, acts_send, acts_recv, cots_send, mate_send, cots_recv, both_recv,
    share_send, share_recv,
):
    wide = lax.axis_index("wide")
    narrow = lax.axis_index("narrow")
    count = n_wide * n_narrow
    me = wide * n_narrow + narrow
    lines = n_wide // (2 * cross)
    core = lax.rem(wide, 2)
    side = lax.rem(wide // 2, cross)
    place = wide // (2 * cross)
    mate = place + 1 - 2 * lax.rem(place, 2)
    tok_acts = acts.shape[0]
    tok_cots = cots.shape[0]
    tokens = acts_all.shape[0]
    rows, cols = bits_in.shape
    row_block = left_ref.shape[0]
    col_block = right_ref.shape[0]
    row_groups = rows // row_block
    per_group = col_block // LANES
    seg_count = len(windows)
    stretch = per_group * rows * seg_count
    blocks, per_block = kept.shape[:2]
    pieces = acts_send.shape[1]
    piece = tok_acts // pieces

    def index_of(at, across, on_core):
        return (at * cross + across) * 2 + on_core

    partner = index_of(place, side, 1 - core)
    up = index_of(lax.rem(place + 1, lines), side, core)
    down = index_of(lax.rem(place + lines - 1, lines), side, core)
    other_side = 1 - side
    over = index_of(place, other_side, core)
    mate_index = index_of(mate, side, core)
    has_up = place < lines - 1
    has_down = place > 0

    my_cots = pl.ds(wide * tok_cots, tok_cots)

    def columns_of(chunk):
        return pl.ds(pl.multiple_of(chunk * col_block, col_block), col_block)

    def own_cots(chunk):
        return pltpu.make_async_copy(
            cots.at[:, columns_of(chunk)], bufs.at[chunk, my_cots, :], local_sem.at[2]
        )

    own_acts = pltpu.make_async_copy(
        acts, acts_all.at[pl.ds(narrow * tok_acts, tok_acts), :], local_sem.at[0]
    )
    own_bits = pltpu.make_async_copy(bits_in, bits_ref, local_sem.at[1])
    own_kept = pltpu.make_async_copy(kept, rows_at, local_sem.at[3])
    for chunk in range(n_chunks):
        own_cots(chunk).start()
    own_kept.start()
    own_acts.start()
    own_bits.start()

    barrier = pltpu.get_barrier_semaphore()

    def address(who):
        return {"wide": who // n_narrow, "narrow": lax.rem(who, n_narrow)}

    def greet(off, _):
        who = lax.rem(me + off, count)
        pl.semaphore_signal(barrier, inc=1, device_id=address(who), device_id_type=MESH)
        return 0

    lax.fori_loop(1, count, greet, 0)
    pl.semaphore_wait(barrier, count - 1)

    def acts_copy(off, part):
        spot = pl.multiple_of(part * piece, piece)
        return pltpu.make_async_remote_copy(
            src_ref=acts.at[pl.ds(spot, piece), :],
            dst_ref=acts_all.at[pl.ds(narrow * tok_acts + spot, piece), :],
            send_sem=acts_send.at[off - 1, part],
            recv_sem=acts_recv.at[off - 1, part],
            device_id={"narrow": lax.rem(narrow + off, n_narrow)},
            device_id_type=MESH,
        )

    def cots_copy(chunk, shard, to, send_sem, own=False):
        place_of = bufs.at[chunk, pl.ds(shard * tok_cots, tok_cots), :]
        return pltpu.make_async_remote_copy(
            src_ref=cots.at[:, columns_of(chunk)] if own else place_of,
            dst_ref=place_of,
            send_sem=send_sem,
            recv_sem=both_recv.at[chunk] if to is partner else cots_recv.at[chunk, shard // 2],
            device_id={"wide": to},
            device_id_type=MESH,
        )

    def turn(chunk):
        return core == lax.rem(chunk, 2)

    def from_own_side(chunk, at, climbs, drops, own=False):
        shard = index_of(at, side, core)
        step = lax.rem(chunk, 2)

        def to_device(way, to):
            return cots_copy(chunk, shard, to, cots_send.at[way, step, at], own)

        todo = [(lambda chunk: ~((at == mate) & turn(chunk)), to_device(3, over))]
        if climbs:
            todo.append((lambda chunk: has_up, to_device(0, up)))
        if drops:
            todo.append((lambda chunk: has_down, to_device(1, down)))
        todo.append((None, to_device(2, partner)))
        return todo

    def from_other_side(chunk, at):
        shard = index_of(at, other_side, core)
        step = lax.rem(chunk, 2)
        return [
            (
                lambda chunk: (at == place) & turn(chunk),
                cots_copy(chunk, shard, mate_index, mate_send.at[step]),
            ),
            (None, cots_copy(chunk, shard, partner, cots_send.at[4, step, at])),
        ]

    def sent(chunk, todo):
        for condition, copy in todo:
            if condition is None:
                copy.wait_send()
            else:
                pl.when(condition(chunk))(copy.wait_send)

    def start(chunk, todo):
        for condition, copy in todo:
            if condition is None:
                pl.when(chunk >= 2)(copy.wait_send)
                copy.start()
            else:
                pl.when((chunk >= 2) & condition(chunk - 2))(copy.wait_send)
                pl.when(condition(chunk))(copy.start)

    def arrived(chunk, shard):
        cots_copy(chunk, shard, up, mate_send.at[0]).wait_recv()

    def along(chunk, step, act, wait):
        @pl.when(place - step >= 0)
        def _():
            if wait:
                arrived(chunk, index_of(place - step, side, core))
            act(from_own_side(chunk, place - step, True, False))

        @pl.when(place + step < lines)
        def _():
            if wait:
                arrived(chunk, index_of(place + step, side, core))
            act(from_own_side(chunk, place + step, False, True))

    def across(chunk, step):
        for way in (1,) if step == 0 else (-1, 1):
            at = place + way * step

            @pl.when((at >= 0) & (at < lines))
            def _():
                arrived(chunk, index_of(at, other_side, core))
                start(chunk, from_other_side(chunk, at))

    def launch(chunk):
        start(chunk, from_own_side(chunk, place, True, True, True))

    starts = []
    total = 0
    for seg in range(seg_count):
        starts.append(total)
        total = total + lengths[seg]
    starts.append(total)

    def flip(begin):
        begin = pl.multiple_of(begin, TILE)
        values = acts_all[pl.ds(begin, TILE), :].astype(jnp.float32).T
        where_at = begin + lax.broadcasted_iota(jnp.int32, values.shape, 1)
        offset = 0
        for seg, (low, high) in enumerate(windows):

            @pl.when((begin >= low) & (begin < high))
            def _():
                inside = (where_at >= starts[seg]) & (where_at < starts[seg + 1])
                spot = pl.multiple_of(offset + begin - low, TILE)
                flipped[:, pl.ds(spot, TILE)] = jnp.where(inside, values, 0.0).astype(jnp.bfloat16)

            offset += high - low

    def flip_own(part, _):
        spot = narrow * tok_acts + part * piece

        def one(at, _):
            flip(spot + at * TILE)
            return 0

        return lax.fori_loop(0, piece // TILE, one, 0)

    def flip_far(part, _):
        for off in range(1, n_narrow):
            acts_copy(off, part).wait_recv()
            spot = lax.rem(narrow + n_narrow - off, n_narrow) * tok_acts + part * piece

            def one(at, _):
                flip(spot + at * TILE)
                return 0

            lax.fori_loop(0, piece // TILE, one, 0)
        return 0

    def prologue():
        left_ref[...] = sylvester(row_block)
        right_ref[...] = sylvester(col_block)
        table[pl.ds(0, PAD), :] = jnp.zeros((PAD, LANES), jnp.float32)
        table[pl.ds(PAD + n_chunks * stretch, PAD), :] = jnp.zeros((PAD, LANES), jnp.float32)
        full_rows, full_cols = full_shape
        scale = 1.0 / math.sqrt(full_rows * full_cols)
        own_kept.wait()
        index = rows_at[...]
        row_of = lax.shift_right_logical(index, log2(full_cols))
        col_of = index & (full_cols - 1)
        common = lax.shift_right_logical(row_of, log2(rows)) & wide
        odd = parity(common) ^ parity(lax.shift_right_logical(col_of, log2(cols)) & narrow)
        signs_at[...] = (1 - 2 * odd).astype(jnp.float32) * scale
        col = col_of & (cols - 1)
        lane_block = lax.shift_right_logical(col, log2(LANES))
        rows_at[...] = (lane_block * rows + (row_of & (rows - 1))) * seg_count
        lanes_at[...] = col & (LANES - 1)

    def multiply(chunk):
        half_rows = bufs.at[chunk, pl.ds(0, tokens // 2), :]
        pltpu.make_async_remote_copy(
            src_ref=half_rows,
            dst_ref=half_rows,
            send_sem=mate_send.at[0],
            recv_sem=both_recv.at[chunk],
            device_id={"wide": partner},
            device_id_type=MESH,
        ).wait_recv()

        columns = columns_of(chunk)
        offset = 0
        for seg, (low, high) in enumerate(windows):
            grads[seg] = jnp.dot(
                flipped[:, offset : offset + high - low],
                bufs[chunk, low:high, :],
                preferred_element_type=jnp.float32,
            )
            offset += high - low

    def transform(chunk):
        columns = columns_of(chunk)
        for seg in range(seg_count):
            gain = lax.rsqrt(jnp.full((1, col_block), lengths[seg], jnp.int32).astype(jnp.float32))
            sign = (1 - 2 * bits_ref[:, columns]).astype(jnp.float32)
            grad = grads[seg] * (sign * gain)
            parts = [
                grad[group * row_block : (group + 1) * row_block]
                for group in range(row_groups)
            ]
            for group, part in enumerate(butterflies(parts)):
                upper, lower = halves(part)
                mixed = jnp.dot(
                    left_ref[...], upper, preferred_element_type=jnp.float32
                ) + jnp.dot(left_ref[...], lower, preferred_element_type=jnp.float32)
                upper, lower = halves(mixed)
                mixed = jnp.dot(
                    upper, right_ref[...], preferred_element_type=jnp.float32
                ) + jnp.dot(lower, right_ref[...], preferred_element_type=jnp.float32)
                for lane_block in range(per_group):
                    block = chunk * per_group + lane_block
                    base = PAD + (block * rows + group * row_block) * seg_count + seg
                    table[pl.ds(base, row_block, stride=seg_count), :] = mixed[
                        :, lane_block * LANES : (lane_block + 1) * LANES
                    ]

    for part in range(pieces):
        for off in range(1, n_narrow):
            acts_copy(off, part).start()

    def inside(chunk):
        return (chunk >= 0) & (chunk < n_chunks)

    def relay(chunk, step):
        @pl.when(inside(chunk))
        def _():
            along(chunk, step, functools.partial(start, chunk), True)

    def accept(chunk, step):
        @pl.when(inside(chunk))
        def _():
            across(chunk, step)

    begun = 3 * (pieces + 3) + 1

    def ready(at, units):
        slot = at // 3 - 2
        reach = jnp.where(at % 3 == 2, slot - lines + 1, slot - lines)
        return (at >= begun) & (units < 2 * n_chunks) & (units // 2 <= reach)

    def work(at, units):
        slot = at // 3 - 2
        phase = at % 3

        @pl.when(phase == 0)
        def _():
            for step in range(min(2, lines - 1), 0, -1):
                if step == min(2, lines - 1):
                    relay(slot - 1, 1)
                accept(slot - 3, step)
            for step in range(lines - 1, 2, -1):
                accept(slot - step, step)

        @pl.when(phase == 1)
        def _():
            accept(slot - 2, 0)

            @pl.when(inside(slot + 2))
            def _():
                launch(slot + 2)

            @pl.when(slot == -2)
            def _():
                prologue()
                own_acts.wait()

            near = slot + 2
            lax.fori_loop(
                lax.clamp(0, near, pieces), lax.clamp(0, near + 1, pieces), flip_own, 0
            )
            far = slot - 2
            lax.fori_loop(lax.clamp(0, far, pieces), lax.clamp(0, far + 1, pieces), flip_far, 0)

            for step in range(lines - 1, 2, -1):
                relay(slot + 1 - step, step)

        @pl.when(phase == 2)
        def _():
            relay(slot - 1, 2)

        @pl.when(at == begun)
        def _():
            own_bits.wait()
            pltpu.make_async_copy(
                bufs.at[:, my_cots, :], bufs.at[:, my_cots, :], local_sem.at[2]
            ).wait()

        go = ready(at, units)
        pl.when(go & (units % 2 == 0))(lambda: multiply(units // 2))
        pl.when(go & (units % 2 == 1))(lambda: transform(units // 2))
        return units + jnp.where(go, 1, 0)

    last, units = 0, 0
    while units < 2 * n_chunks or last < 3 * (n_chunks + lines + 1) + 1:
        slot = last // 3 - 2
        reach = slot - lines + 1 if last % 3 == 2 else slot - lines
        if last >= begun and units < 2 * n_chunks and units // 2 <= reach:
            units += 1
        last += 1
    lax.fori_loop(0, last, work, 0)

    def fetch(block, half):
        return pltpu.make_async_copy(rows_at.at[block], spots.at[half], spots_sem.at[half])

    def block_at(turn_at):
        return lax.rem(me + turn_at + 1, count) if scatter else turn_at

    for half in range(BUFFERS):
        fetch(block_at(half), half).start()

    def join(at, _):
        base = pl.multiple_of(PAD + at * 8, 8)
        spans = [pl.ds(base + chunk * stretch, 8) for chunk in range(n_chunks)]
        parts = butterflies([table[span, :] for span in spans])
        for span, part in zip(spans, parts):
            table[span, :] = part
        return 0

    lax.fori_loop(0, stretch // 8, join, 0, unroll=8)

    lane = lax.broadcasted_iota(jnp.int32, (8, LANES), 1)
    row = lax.broadcasted_iota(jnp.int32, (8, LANES), 0)
    first = row < seg_count
    place_in = lane & (HALF - 1)

    def share_copy(who, slot):
        return pltpu.make_async_remote_copy(
            src_ref=shares.at[who],
            dst_ref=held.at[slot],
            send_sem=share_send,
            recv_sem=share_recv,
            device_id=address(who),
            device_id_type=MESH,
        )

    def pick_block(block, half):
        for group in range(per_block):
            lanes = jnp.broadcast_to(lanes_at[block, group : group + 1, :], (8, LANES))
            found = [jnp.zeros((8, LANES), jnp.float32)] * 2
            for at in range(HALF):
                one = spots[half, group, at]
                two = spots[half, group, at + HALF]
                values = jnp.where(
                    first, table[pl.ds(one + PAD, 8), :], table[pl.ds(two + PAD - seg_count, 8), :]
                )
                values = jnp.take_along_axis(values, lanes, axis=1)
                found[at % 2] = jnp.where(place_in == at, values, found[at % 2])
            both = found[0] + found[1]
            picked = jnp.where(
                lane[:seg_count] < HALF, both[:seg_count], both[seg_count : 2 * seg_count]
            )
            shares[block, group * seg_count : (group + 1) * seg_count, :] = (
                picked * signs_at[block, group : group + 1, :]
            )

    def pick(pair, _):
        for run in range(2):
            halves_at = range(run * RUN, (run + 1) * RUN)
            for half in halves_at:
                fetch(block_at(pair * BUFFERS + half), half).wait()
            for half in halves_at:
                pick_block(block_at(pair * BUFFERS + half), half)

            @pl.when(pair + 1 < blocks // BUFFERS)
            def _():
                for half in halves_at:
                    fetch(block_at((pair + 1) * BUFFERS + half), half).start()

            if scatter:
                for half in halves_at:
                    turn_at = pair * BUFFERS + half

                    @pl.when(turn_at + 1 < count)
                    def _():
                        share_copy(block_at(turn_at), me).start()
        return 0

    lax.fori_loop(0, blocks // BUFFERS, pick, 0)

    def finish(chunk, _):
        sent(chunk, from_own_side(chunk, place, True, True, True))
        for step in range(1, lines):
            along(chunk, step, functools.partial(sent, chunk), False)
        for at in range(lines):
            sent(chunk, from_other_side(chunk, at))
        return 0

    lax.fori_loop(max(0, n_chunks - 2), n_chunks, finish, 0)
    for part in range(pieces):
        for off in range(1, n_narrow):
            acts_copy(off, part).wait_send()


    if scatter:

        def take(off, total):
            return total + held[lax.rem(me + off, count)]

        others = pl.ds(0, count - 1)
        all_shares = pltpu.make_async_remote_copy(
            src_ref=shares.at[others],
            dst_ref=held.at[others],
            send_sem=share_send,
            recv_sem=share_recv,
            device_id=address(me),
            device_id_type=MESH,
        )
        all_shares.wait_recv()
        total = lax.fori_loop(1, count, take, shares[me])
        for group in range(per_block):
            out_ref[:, group * LANES : (group + 1) * LANES] = total[
                group * seg_count : (group + 1) * seg_count
            ]

        all_shares.wait_send()
    else:
        out_ref[...] = shares[...]


def body(n_wide, n_narrow, activations, cotangent, sign_bits, seg_lengths, kept_index):
    tokens = activations.shape[0] * n_narrow
    rows, cols = sign_bits.shape
    seg_count = seg_lengths.shape[0]
    kept = kept_index.shape[0]
    count = n_wide * n_narrow
    each = kept // count
    scatter = each % LANES == 0
    per_block = each // LANES if scatter else 4
    blocks = kept // LANES // per_block
    cross = 2
    row_block, col_block = min(rows, 256), min(cols, 256)
    n_chunks = cols // col_block
    windows = []
    for seg in range(seg_count):
        low = max(0, tokens - (seg_count - seg) * MOST) // TILE * TILE
        high = min(tokens, -(-(seg + 1) * MOST // TILE) * TILE)
        windows.append((low, high))
    pieces = max(1, activations.shape[0] // 512)
    anywhere = pl.BlockSpec(memory_space=pl.ANY)
    scalars = pl.BlockSpec(memory_space=pltpu.SMEM)
    vectors = pl.BlockSpec(memory_space=pltpu.VMEM)
    table = rows * cols // LANES * seg_count + 2 * PAD
    block_shape = (blocks, per_block, LANES)
    share_shape = (blocks, per_block * seg_count, LANES)
    out = (seg_count, each) if scatter else share_shape
    shares = pl.pallas_call(
        functools.partial(
            sketch_kernel, n_wide, n_narrow, cross, tuple(windows), n_chunks, scatter,
            (rows * n_wide, cols * n_narrow),
        ),
        out_shape=jax.ShapeDtypeStruct(out, jnp.float32),
        in_specs=[scalars] + [anywhere] * 4,
        out_specs=vectors,
        scratch_shapes=[
            pltpu.VMEM((tokens, rows), activations.dtype),
            pltpu.VMEM((rows, cols), sign_bits.dtype),
            pltpu.VMEM((rows, sum(high - low for low, high in windows)), jnp.bfloat16),
            pltpu.VMEM((table, LANES), jnp.float32),
            pltpu.VMEM((n_chunks, cotangent.shape[0] * n_wide, col_block), cotangent.dtype),
            pltpu.VMEM((seg_count, rows, col_block), jnp.float32),
            pltpu.VMEM((row_block, row_block), jnp.bfloat16),
            pltpu.VMEM((col_block, col_block), jnp.bfloat16),
            pltpu.VMEM(block_shape, jnp.int32),
            pltpu.VMEM(block_shape, jnp.int32),
            pltpu.VMEM(block_shape, jnp.float32),
            pltpu.SMEM((BUFFERS, per_block, LANES), jnp.int32),
            pltpu.VMEM(share_shape, jnp.float32),
            pltpu.VMEM(share_shape, jnp.float32),
            pltpu.SemaphoreType.DMA((4,)),
            pltpu.SemaphoreType.DMA((BUFFERS,)),
            pltpu.SemaphoreType.DMA((max(1, n_narrow - 1), pieces)),
            pltpu.SemaphoreType.DMA((max(1, n_narrow - 1), pieces)),
            pltpu.SemaphoreType.DMA((5, 2, n_wide // (2 * cross))),
            pltpu.SemaphoreType.DMA((2,)),
            pltpu.SemaphoreType.DMA((n_chunks, n_wide // 2)),
            pltpu.SemaphoreType.DMA((n_chunks,)),
            pltpu.SemaphoreType.DMA,
            pltpu.SemaphoreType.DMA,
        ],
        compiler_params=pltpu.CompilerParams(
            collective_id=0, has_side_effects=True, vmem_limit_bytes=62 * 1024 * 1024
        ),
        name="sketch",
    )(seg_lengths, kept_index.reshape(block_shape), activations, cotangent, sign_bits)
    if scatter:
        return shares
    flat = shares.reshape(blocks, per_block, seg_count, LANES)
    flat = flat.transpose(2, 0, 1, 3).reshape(seg_count, kept)
    return lax.psum_scatter(flat, ("wide", "narrow"), scatter_dimension=1, tiled=True)


def solution(mesh):
    return jax.shard_map(
        functools.partial(body, mesh.shape["wide"], mesh.shape["narrow"]),
        mesh=mesh,
        in_specs=(P("narrow", "wide"), P("wide", "narrow"), P("wide", "narrow"), P(), P()),
        out_specs=P(None, ("wide", "narrow")),
        check_vma=False,
    )
```

```python
import functools
import math

import jax
import jax.numpy as jnp
from jax import lax
from jax.experimental import pallas as pl
from jax.experimental.pallas import tpu as pltpu
from jax.sharding import PartitionSpec as P

LANES = 128
HALF = LANES // 2
MOST = 1536
TILE = 256
PAD = 8
RUN = 2
BUFFERS = 2 * RUN
MESH = pl.DeviceIdType.MESH


def parity(values):
    for shift in (16, 8, 4, 2, 1):
        values = values ^ lax.shift_right_logical(values, shift)
    return values & 1


def sylvester(extent):
    rows = lax.broadcasted_iota(jnp.int32, (extent, extent), 0)
    cols = lax.broadcasted_iota(jnp.int32, (extent, extent), 1)
    return (1 - 2 * parity(rows & cols)).astype(jnp.float32).astype(jnp.bfloat16)


def butterflies(parts):
    parts = list(parts)
    gap = 1
    while gap < len(parts):
        for low in range(len(parts)):
            if not low & gap:
                one, two = parts[low], parts[low | gap]
                parts[low], parts[low | gap] = one + two, one - two
        gap *= 2
    return parts


def halves(values):
    high = values.astype(jnp.bfloat16)
    low = (values - high.astype(jnp.float32)).astype(jnp.bfloat16)
    return high, low


def log2(extent):
    return extent.bit_length() - 1


def sketch_kernel(
    n_wide, n_narrow, cross, windows, n_chunks, scatter, full_shape,
    lengths, kept, acts, cots, bits_in,
    out_ref, acts_all, bits_ref, flipped, table, bufs, grads, left_ref, right_ref,
    rows_at, lanes_at, signs_at, spots, shares, held,
    local_sem, spots_sem, acts_send, acts_recv, cots_send, mate_send, cots_recv, both_recv,
    share_send, share_recv,
):
    wide = lax.axis_index("wide")
    narrow = lax.axis_index("narrow")
    count = n_wide * n_narrow
    me = wide * n_narrow + narrow
    lines = n_wide // (2 * cross)
    core = lax.rem(wide, 2)
    side = lax.rem(wide // 2, cross)
    place = wide // (2 * cross)
    mate = place + 1 - 2 * lax.rem(place, 2)
    tok_acts = acts.shape[0]
    tok_cots = cots.shape[0]
    tokens = acts_all.shape[0]
    rows, cols = bits_in.shape
    row_block = left_ref.shape[0]
    col_block = right_ref.shape[0]
    row_groups = rows // row_block
    per_group = col_block // LANES
    seg_count = len(windows)
    stretch = per_group * rows * seg_count
    blocks, per_block = kept.shape[:2]
    pieces = acts_send.shape[1]
    piece = tok_acts // pieces

    def index_of(at, across, on_core):
        return (at * cross + across) * 2 + on_core

    partner = index_of(place, side, 1 - core)
    up = index_of(lax.rem(place + 1, lines), side, core)
    down = index_of(lax.rem(place + lines - 1, lines), side, core)
    other_side = 1 - side
    over = index_of(place, other_side, core)
    mate_index = index_of(mate, side, core)
    has_up = place < lines - 1
    has_down = place > 0

    my_cots = pl.ds(wide * tok_cots, tok_cots)

    def columns_of(chunk):
        return pl.ds(pl.multiple_of(chunk * col_block, col_block), col_block)

    def own_cots(chunk):
        return pltpu.make_async_copy(
            cots.at[:, columns_of(chunk)], bufs.at[chunk, my_cots, :], local_sem.at[2]
        )

    own_acts = pltpu.make_async_copy(
        acts, acts_all.at[pl.ds(narrow * tok_acts, tok_acts), :], local_sem.at[0]
    )
    own_bits = pltpu.make_async_copy(bits_in, bits_ref, local_sem.at[1])
    own_kept = pltpu.make_async_copy(kept, rows_at, local_sem.at[3])
    own_kept.start()

    barrier = pltpu.get_barrier_semaphore()

    def address(who):
        return {"wide": who // n_narrow, "narrow": lax.rem(who, n_narrow)}

    def greet(off, _):
        who = lax.rem(me + off, count)
        pl.semaphore_signal(barrier, inc=1, device_id=address(who), device_id_type=MESH)
        return 0

    lax.fori_loop(1, count, greet, 0)
    pl.semaphore_wait(barrier, count - 1)

    def acts_copy(off, part):
        spot = pl.multiple_of(part * piece, piece)
        return pltpu.make_async_remote_copy(
            src_ref=acts.at[pl.ds(spot, piece), :],
            dst_ref=acts_all.at[pl.ds(narrow * tok_acts + spot, piece), :],
            send_sem=acts_send.at[off - 1, part],
            recv_sem=acts_recv.at[off - 1, part],
            device_id={"narrow": lax.rem(narrow + off, n_narrow)},
            device_id_type=MESH,
        )

    def cots_copy(chunk, shard, to, send_sem, own=False):
        place_of = bufs.at[chunk, pl.ds(shard * tok_cots, tok_cots), :]
        return pltpu.make_async_remote_copy(
            src_ref=cots.at[:, columns_of(chunk)] if own else place_of,
            dst_ref=place_of,
            send_sem=send_sem,
            recv_sem=both_recv.at[chunk] if to is partner else cots_recv.at[chunk, shard // 2],
            device_id={"wide": to},
            device_id_type=MESH,
        )

    def turn(chunk):
        return (core == lax.rem(chunk, 2)) & (chunk != n_chunks // 2)

    def from_own_side(chunk, at, climbs, drops, own=False):
        shard = index_of(at, side, core)
        step = lax.rem(chunk, 2)

        def to_device(way, to):
            return cots_copy(chunk, shard, to, cots_send.at[way, step, at], own)

        todo = [(lambda chunk: ~((at == mate) & turn(chunk)), to_device(3, over))]
        if climbs:
            todo.append((lambda chunk: has_up, to_device(0, up)))
        if drops:
            todo.append((lambda chunk: has_down, to_device(1, down)))
        todo.append((None, to_device(2, partner)))
        return todo

    def from_other_side(chunk, at):
        shard = index_of(at, other_side, core)
        step = lax.rem(chunk, 2)
        return [
            (
                lambda chunk: (at == place) & turn(chunk),
                cots_copy(chunk, shard, mate_index, mate_send.at[step]),
            ),
            (None, cots_copy(chunk, shard, partner, cots_send.at[4, step, at])),
        ]

    def sent(chunk, todo):
        for condition, copy in todo:
            if condition is None:
                copy.wait_send()
            else:
                pl.when(condition(chunk))(copy.wait_send)

    def start(chunk, todo):
        for condition, copy in todo:
            if condition is None:
                pl.when(chunk >= 2)(copy.wait_send)
                copy.start()
            else:
                pl.when((chunk >= 2) & condition(chunk - 2))(copy.wait_send)
                pl.when(condition(chunk))(copy.start)

    def arrived(chunk, shard):
        cots_copy(chunk, shard, up, mate_send.at[0]).wait_recv()

    def along(chunk, step, act, wait):
        @pl.when(place - step >= 0)
        def _():
            if wait:
                arrived(chunk, index_of(place - step, side, core))
            act(from_own_side(chunk, place - step, True, False))

        @pl.when(place + step < lines)
        def _():
            if wait:
                arrived(chunk, index_of(place + step, side, core))
            act(from_own_side(chunk, place + step, False, True))

    def across(chunk, step):
        for way in (1,) if step == 0 else (-1, 1):
            at = place + way * step

            @pl.when((at >= 0) & (at < lines))
            def _():
                arrived(chunk, index_of(at, other_side, core))
                start(chunk, from_other_side(chunk, at))

    def launch(chunk):
        start(chunk, from_own_side(chunk, place, True, True, True))

    starts = []
    total = 0
    for seg in range(seg_count):
        starts.append(total)
        total = total + lengths[seg]
    starts.append(total)

    def flip(begin):
        begin = pl.multiple_of(begin, TILE)
        values = acts_all[pl.ds(begin, TILE), :].astype(jnp.float32).T
        where_at = begin + lax.broadcasted_iota(jnp.int32, values.shape, 1)
        offset = 0
        for seg, (low, high) in enumerate(windows):

            @pl.when((begin >= low) & (begin < high))
            def _():
                inside = (where_at >= starts[seg]) & (where_at < starts[seg + 1])
                spot = pl.multiple_of(offset + begin - low, TILE)
                flipped[:, pl.ds(spot, TILE)] = jnp.where(inside, values, 0.0).astype(jnp.bfloat16)

            offset += high - low

    def flip_own(part, _):
        spot = narrow * tok_acts + part * piece

        def one(at, _):
            flip(spot + at * TILE)
            return 0

        return lax.fori_loop(0, piece // TILE, one, 0)

    def flip_far(part, _):
        for off in range(1, n_narrow):
            acts_copy(off, part).wait_recv()
            spot = lax.rem(narrow + n_narrow - off, n_narrow) * tok_acts + part * piece

            def one(at, _):
                flip(spot + at * TILE)
                return 0

            lax.fori_loop(0, piece // TILE, one, 0)
        return 0

    def prologue():
        left_ref[...] = sylvester(row_block)
        right_ref[...] = sylvester(col_block)
        table[pl.ds(0, PAD), :] = jnp.zeros((PAD, LANES), jnp.float32)
        table[pl.ds(PAD + n_chunks * stretch, PAD), :] = jnp.zeros((PAD, LANES), jnp.float32)
        full_rows, full_cols = full_shape
        scale = 1.0 / math.sqrt(full_rows * full_cols)
        own_kept.wait()
        index = rows_at[...]
        row_of = lax.shift_right_logical(index, log2(full_cols))
        col_of = index & (full_cols - 1)
        common = lax.shift_right_logical(row_of, log2(rows)) & wide
        odd = parity(common) ^ parity(lax.shift_right_logical(col_of, log2(cols)) & narrow)
        signs_at[...] = (1 - 2 * odd).astype(jnp.float32) * scale
        col = col_of & (cols - 1)
        lane_block = lax.shift_right_logical(col, log2(LANES))
        rows_at[...] = (lane_block * rows + (row_of & (rows - 1))) * seg_count
        lanes_at[...] = col & (LANES - 1)

    def multiply(chunk):
        half_rows = bufs.at[chunk, pl.ds(0, tokens // 2), :]
        pltpu.make_async_remote_copy(
            src_ref=half_rows,
            dst_ref=half_rows,
            send_sem=mate_send.at[0],
            recv_sem=both_recv.at[chunk],
            device_id={"wide": partner},
            device_id_type=MESH,
        ).wait_recv()

        columns = columns_of(chunk)
        offset = 0
        for seg, (low, high) in enumerate(windows):
            grads[seg] = jnp.dot(
                flipped[:, offset : offset + high - low],
                bufs[chunk, low:high, :],
                preferred_element_type=jnp.float32,
            )
            offset += high - low

    def transform(chunk):
        columns = columns_of(chunk)
        for seg in range(seg_count):
            gain = lax.rsqrt(jnp.full((1, col_block), lengths[seg], jnp.int32).astype(jnp.float32))
            sign = (1 - 2 * bits_ref[:, columns]).astype(jnp.float32)
            grad = grads[seg] * (sign * gain)
            parts = [
                grad[group * row_block : (group + 1) * row_block]
                for group in range(row_groups)
            ]
            for group, part in enumerate(butterflies(parts)):
                upper, lower = halves(part)
                mixed = jnp.dot(
                    left_ref[...], upper, preferred_element_type=jnp.float32
                ) + jnp.dot(left_ref[...], lower, preferred_element_type=jnp.float32)
                upper, lower = halves(mixed)
                mixed = jnp.dot(
                    upper, right_ref[...], preferred_element_type=jnp.float32
                ) + jnp.dot(lower, right_ref[...], preferred_element_type=jnp.float32)
                for lane_block in range(per_group):
                    block = chunk * per_group + lane_block
                    base = PAD + (block * rows + group * row_block) * seg_count + seg
                    table[pl.ds(base, row_block, stride=seg_count), :] = mixed[
                        :, lane_block * LANES : (lane_block + 1) * LANES
                    ]

    for part in range(pieces):
        for off in range(1, n_narrow):
            acts_copy(off, part).start()

    def inside(chunk):
        return (chunk >= 0) & (chunk < n_chunks)

    def relay(chunk, step):
        @pl.when(inside(chunk))
        def _():
            along(chunk, step, functools.partial(start, chunk), True)

    def accept(chunk, step):
        @pl.when(inside(chunk))
        def _():
            across(chunk, step)

    begun = 3 * (pieces + 3) + 1

    def ready(at, units):
        slot = at // 3 - 2
        reach = jnp.where(at % 3 == 2, slot - lines + 1, slot - lines)
        return (at >= begun) & (units < 2 * n_chunks) & (units // 2 <= reach)

    def work(at, units):
        slot = at // 3 - 2
        phase = at % 3

        @pl.when(phase == 0)
        def _():
            for step in range(min(2, lines - 1), 0, -1):
                if step == min(2, lines - 1):
                    relay(slot - 1, 1)
                accept(slot - 3, step)
            for step in range(lines - 1, 2, -1):
                accept(slot - step, step)

        @pl.when(phase == 1)
        def _():
            accept(slot - 2, 0)

            @pl.when(inside(slot + 2))
            def _():
                launch(slot + 2)

            @pl.when(slot == -2)
            def _():
                own_acts.start()
                prologue()
                own_acts.wait()
                for chunk in range(n_chunks):
                    own_cots(chunk).start()
                own_bits.start()

            near = slot + 2
            lax.fori_loop(
                lax.clamp(0, near, pieces), lax.clamp(0, near + 1, pieces), flip_own, 0
            )
            far = slot - 2
            lax.fori_loop(lax.clamp(0, far, pieces), lax.clamp(0, far + 1, pieces), flip_far, 0)

            for step in range(lines - 1, 2, -1):
                relay(slot + 1 - step, step)

        @pl.when(phase == 2)
        def _():
            relay(slot - 1, 2)

        @pl.when(at == begun)
        def _():
            own_bits.wait()
            pltpu.make_async_copy(
                bufs.at[:, my_cots, :], bufs.at[:, my_cots, :], local_sem.at[2]
            ).wait()

        go = ready(at, units)
        pl.when(go & (units % 2 == 0))(lambda: multiply(units // 2))
        pl.when(go & (units % 2 == 1))(lambda: transform(units // 2))
        return units + jnp.where(go, 1, 0)

    last, units = 0, 0
    while units < 2 * n_chunks or last < 3 * (n_chunks + lines + 1) + 1:
        slot = last // 3 - 2
        reach = slot - lines + 1 if last % 3 == 2 else slot - lines
        if last >= begun and units < 2 * n_chunks and units // 2 <= reach:
            units += 1
        last += 1
    lax.fori_loop(0, last, work, 0)

    def fetch(block, half):
        return pltpu.make_async_copy(rows_at.at[block], spots.at[half], spots_sem.at[half])

    def block_at(turn_at):
        return lax.rem(me + turn_at + 1, count) if scatter else turn_at

    for half in range(BUFFERS):
        fetch(block_at(half), half).start()

    def join(at, _):
        base = pl.multiple_of(PAD + at * 8, 8)
        spans = [pl.ds(base + chunk * stretch, 8) for chunk in range(n_chunks)]
        parts = butterflies([table[span, :] for span in spans])
        for span, part in zip(spans, parts):
            table[span, :] = part
        return 0

    lax.fori_loop(0, stretch // 8, join, 0, unroll=8)

    lane = lax.broadcasted_iota(jnp.int32, (8, LANES), 1)
    row = lax.broadcasted_iota(jnp.int32, (8, LANES), 0)
    first = row < seg_count
    place_in = lane & (HALF - 1)

    def share_copy(who, slot):
        return pltpu.make_async_remote_copy(
            src_ref=shares.at[who],
            dst_ref=held.at[slot],
            send_sem=share_send,
            recv_sem=share_recv,
            device_id=address(who),
            device_id_type=MESH,
        )

    def pick_block(block, half):
        for group in range(per_block):
            lanes = jnp.broadcast_to(lanes_at[block, group : group + 1, :], (8, LANES))
            found = [jnp.zeros((8, LANES), jnp.float32)] * 2
            for at in range(HALF):
                one = spots[half, group, at]
                two = spots[half, group, at + HALF]
                values = jnp.where(
                    first, table[pl.ds(one + PAD, 8), :], table[pl.ds(two + PAD - seg_count, 8), :]
                )
                values = jnp.take_along_axis(values, lanes, axis=1)
                found[at % 2] = jnp.where(place_in == at, values, found[at % 2])
            both = found[0] + found[1]
            picked = jnp.where(
                lane[:seg_count] < HALF, both[:seg_count], both[seg_count : 2 * seg_count]
            )
            shares[block, group * seg_count : (group + 1) * seg_count, :] = (
                picked * signs_at[block, group : group + 1, :]
            )

    def pick(pair, _):
        for run in range(2):
            halves_at = range(run * RUN, (run + 1) * RUN)
            for half in halves_at:
                fetch(block_at(pair * BUFFERS + half), half).wait()
            for half in halves_at:
                pick_block(block_at(pair * BUFFERS + half), half)

            @pl.when(pair + 1 < blocks // BUFFERS)
            def _():
                for half in halves_at:
                    fetch(block_at((pair + 1) * BUFFERS + half), half).start()

            if scatter:
                for half in halves_at:
                    turn_at = pair * BUFFERS + half

                    @pl.when(turn_at + 1 < count)
                    def _():
                        share_copy(block_at(turn_at), me).start()
        return 0

    lax.fori_loop(0, blocks // BUFFERS, pick, 0)

    def finish(chunk, _):
        sent(chunk, from_own_side(chunk, place, True, True, True))
        for step in range(1, lines):
            along(chunk, step, functools.partial(sent, chunk), False)
        for at in range(lines):
            sent(chunk, from_other_side(chunk, at))
        return 0

    lax.fori_loop(max(0, n_chunks - 2), n_chunks, finish, 0)
    for part in range(pieces):
        for off in range(1, n_narrow):
            acts_copy(off, part).wait_send()


    if scatter:

        def take(off, total):
            return total + held[lax.rem(me + off, count)]

        others = pl.ds(0, count - 1)
        all_shares = pltpu.make_async_remote_copy(
            src_ref=shares.at[others],
            dst_ref=held.at[others],
            send_sem=share_send,
            recv_sem=share_recv,
            device_id=address(me),
            device_id_type=MESH,
        )
        all_shares.wait_recv()
        total = lax.fori_loop(1, count, take, shares[me])
        for group in range(per_block):
            out_ref[:, group * LANES : (group + 1) * LANES] = total[
                group * seg_count : (group + 1) * seg_count
            ]

        all_shares.wait_send()
    else:
        out_ref[...] = shares[...]


def body(n_wide, n_narrow, activations, cotangent, sign_bits, seg_lengths, kept_index):
    tokens = activations.shape[0] * n_narrow
    rows, cols = sign_bits.shape
    seg_count = seg_lengths.shape[0]
    kept = kept_index.shape[0]
    count = n_wide * n_narrow
    each = kept // count
    scatter = each % LANES == 0
    per_block = each // LANES if scatter else 4
    blocks = kept // LANES // per_block
    cross = 2
    row_block, col_block = min(rows, 256), min(cols, 256)
    n_chunks = cols // col_block
    windows = []
    for seg in range(seg_count):
        low = max(0, tokens - (seg_count - seg) * MOST) // TILE * TILE
        high = min(tokens, -(-(seg + 1) * MOST // TILE) * TILE)
        windows.append((low, high))
    pieces = max(1, activations.shape[0] // 512)
    anywhere = pl.BlockSpec(memory_space=pl.ANY)
    scalars = pl.BlockSpec(memory_space=pltpu.SMEM)
    vectors = pl.BlockSpec(memory_space=pltpu.VMEM)
    table = rows * cols // LANES * seg_count + 2 * PAD
    block_shape = (blocks, per_block, LANES)
    share_shape = (blocks, per_block * seg_count, LANES)
    out = (seg_count, each) if scatter else share_shape
    shares = pl.pallas_call(
        functools.partial(
            sketch_kernel, n_wide, n_narrow, cross, tuple(windows), n_chunks, scatter,
            (rows * n_wide, cols * n_narrow),
        ),
        out_shape=jax.ShapeDtypeStruct(out, jnp.float32),
        in_specs=[scalars] + [anywhere] * 4,
        out_specs=vectors,
        scratch_shapes=[
            pltpu.VMEM((tokens, rows), activations.dtype),
            pltpu.VMEM((rows, cols), sign_bits.dtype),
            pltpu.VMEM((rows, sum(high - low for low, high in windows)), jnp.bfloat16),
            pltpu.VMEM((table, LANES), jnp.float32),
            pltpu.VMEM((n_chunks, cotangent.shape[0] * n_wide, col_block), cotangent.dtype),
            pltpu.VMEM((seg_count, rows, col_block), jnp.float32),
            pltpu.VMEM((row_block, row_block), jnp.bfloat16),
            pltpu.VMEM((col_block, col_block), jnp.bfloat16),
            pltpu.VMEM(block_shape, jnp.int32),
            pltpu.VMEM(block_shape, jnp.int32),
            pltpu.VMEM(block_shape, jnp.float32),
            pltpu.SMEM((BUFFERS, per_block, LANES), jnp.int32),
            pltpu.VMEM(share_shape, jnp.float32),
            pltpu.VMEM(share_shape, jnp.float32),
            pltpu.SemaphoreType.DMA((4,)),
            pltpu.SemaphoreType.DMA((BUFFERS,)),
            pltpu.SemaphoreType.DMA((max(1, n_narrow - 1), pieces)),
            pltpu.SemaphoreType.DMA((max(1, n_narrow - 1), pieces)),
            pltpu.SemaphoreType.DMA((5, 2, n_wide // (2 * cross))),
            pltpu.SemaphoreType.DMA((2,)),
            pltpu.SemaphoreType.DMA((n_chunks, n_wide // 2)),
            pltpu.SemaphoreType.DMA((n_chunks,)),
            pltpu.SemaphoreType.DMA,
            pltpu.SemaphoreType.DMA,
        ],
        compiler_params=pltpu.CompilerParams(
            collective_id=0, has_side_effects=True, vmem_limit_bytes=62 * 1024 * 1024
        ),
        name="sketch",
    )(seg_lengths, kept_index.reshape(block_shape), activations, cotangent, sign_bits)
    if scatter:
        return shares
    flat = shares.reshape(blocks, per_block, seg_count, LANES)
    flat = flat.transpose(2, 0, 1, 3).reshape(seg_count, kept)
    return lax.psum_scatter(flat, ("wide", "narrow"), scatter_dimension=1, tiled=True)


def solution(mesh):
    return jax.shard_map(
        functools.partial(body, mesh.shape["wide"], mesh.shape["narrow"]),
        mesh=mesh,
        in_specs=(P("narrow", "wide"), P("wide", "narrow"), P("wide", "narrow"), P(), P()),
        out_specs=P(None, ("wide", "narrow")),
        check_vma=False,
    )
```
